32 devices in a mesh: gx: 8 (over y, x, core), gy: 4 (over z).
Axes of the slice: x: 2, y: 2, z: 4, core: 2. Of those that a mesh axis runs over, the one named last changes fastest.
Arguments:
- e_field: float32 [3, 3, 2048, 2048], P(None, None, 'gx', 'gy'), may hold values from -6 to 6
- h_field: float32 [3, 3, 2048, 2048], P(None, None, 'gx', 'gy'), may hold values from -6 to 6
- material: int32 [3, 2048, 2048], P(None, 'gx', 'gy'), may hold values from 0 to 7
- eps_table: float32 [8], replicated, may hold values from 1 to 12
- src_pos: int32 [1024, 3], replicated, may hold values from 0 to 2047, as said below
- src_amp: float32 [1024], replicated, may hold values from -40 to 40
- freqs: float32 [2], replicated, may hold values from 0.3 to 2.8
Outputs:
- e_out: float32 [3, 3, 2048, 2048], P(None, None, 'gx', 'gy')
- h_out: float32 [3, 3, 2048, 2048], P(None, None, 'gx', 'gy')
- far_field: float32 [1024, 8, 2, 1024], P('gx', None, None, 'gy')
The draws below stay inside these ranges and needn't reach their ends.
Inputs may be any that keep to these rules, and one draw needn't show every extreme that they name: `src_pos`: each row is a cell (layer, row, column) of the slab; several sources may share a cell.
All inputs are finite; a program needn't handle non-finite values.
Results may differ from the reference program's by a relative error of at most 0.0054.
Values may be sent and summed in bfloat16 or wider, within the bound.
A program may use at most 192 MiB of HBM per device.

```python
import math
import jax
import jax.numpy as jnp
from jax import lax

NX = 2048
NY = 2048
LZ = 3
FACE = 1
STEPS = 2
NF = 2
ITEMS = 8
NA = 1024
NMAT = 8
NSRC = 1024


def draw_src_pos(key, part):
    key_layer, key_row, key_col = jax.random.split(jax.random.fold_in(key, 17), 3)
    layers = jax.random.randint(key_layer, (NSRC,), 0, LZ)
    rows_drawn = jax.random.randint(key_row, (NSRC,), 0, NX)
    cols_drawn = jax.random.randint(key_col, (NSRC,), 0, NY)
    positions = jnp.stack([layers, rows_drawn, cols_drawn], 1).astype(jnp.int32)
    corner = jnp.array([0, NX - 1, NY - 1], jnp.int32)
    return positions.at[0].set(corner)


def place_ends(entries, stream_key, low, high):
    index_at = [jax.random.randint(jax.random.fold_in(stream_key, axis), (), 0, length) for axis, length in enumerate(entries.shape)]
    widest = entries.shape.index(max(entries.shape))
    next_to = index_at[:widest] + [(index_at[widest] + 1) % entries.shape[widest]] + index_at[widest + 1:]
    return entries.at[tuple(index_at)].set(low).at[tuple(next_to)].set(high)


def levels(stream_key, shape, cuts, smallest, high):
    level = 1.0
    for position, parts in cuts:
        heights = jax.random.uniform(jax.random.fold_in(jax.random.fold_in(stream_key, 6), position), (parts,), jnp.float32, smallest / len(cuts), high / len(cuts))
        level = level * jnp.repeat(jnp.exp(heights), shape[position] // parts).reshape((-1,) + (1,) * (len(shape) - 1 - position))
    return level


def normal_values(rng, dims, spread, reach, shards=(), held_as=jnp.bfloat16):
    drawn = jax.random.normal(rng, dims, jnp.float32) * spread
    if len(shards) > 0:
        drawn = levels(rng, dims, shards, -0.22, 0.18) * drawn
    return jnp.clip(drawn, min=-reach, max=reach).astype(held_as)


def setup_inputs(seed: int = 0) -> dict:
    key_list = jax.random.split(jax.random.key(seed), 8)
    e_field = normal_values(key_list[0], (3, LZ, NX, NY), 1.0, 6.0, ((2, 8), (3, 4)), jnp.float32)
    h_field = normal_values(key_list[1], (3, LZ, NX, NY), 1.0, 6.0, ((2, 8), (3, 4)), jnp.float32)
    material = place_ends(jax.random.randint(key_list[2], (LZ, NX, NY), 0, NMAT), jax.random.fold_in(key_list[2], 1), 0, NMAT - 1).astype(jnp.int32)
    eps_table = jnp.clip(jnp.exp(jax.random.uniform(key_list[3], (NMAT,), jnp.float32, math.log(1.0), math.log(12.0))), 1.0, 12.0)
    src_pos = draw_src_pos(jax.random.fold_in(key_list[7], 71), 0)
    src_amp = normal_values(key_list[5], (NSRC,), 8.0, 40.0, (), jnp.float32)
    freqs = jnp.clip(jax.random.uniform(key_list[6], (NF,), jnp.float32, 0.3, 2.8), 0.3, 2.8)
    return {"e_field": e_field, "h_field": h_field, "material": material, "eps_table": eps_table, "src_pos": src_pos, "src_amp": src_amp, "freqs": freqs}


courant = 0.5
source_rate = 0.7
zoom_factor = 4

def chirp(freq_index, cell_index, period):
    remainder = jnp.remainder(freq_index * cell_index, period)
    phase_angle = remainder.astype(jnp.float32) * (2.0 * math.pi / period)
    return (jnp.cos(phase_angle), -jnp.sin(phase_angle))

def forward(field, dimension, boundary):
    inner = lax.slice_in_dim(field, 1, field.shape[dimension], axis=dimension)
    return jnp.concatenate([inner, jnp.expand_dims(boundary, dimension)], dimension)

def backward(field, dimension, boundary):
    inner = lax.slice_in_dim(field, 0, field.shape[dimension] - 1, axis=dimension)
    return jnp.concatenate([jnp.expand_dims(boundary, dimension), inner], dimension)

def curl_forward(electric, row_rim, col_rim):
    field_x, field_y, field_z = (electric[0], electric[1], electric[2])
    zero_layer = jnp.zeros(field_x.shape[1:], jnp.float32)
    curl_x = forward(field_z, 2, col_rim[1]) - field_z - (forward(field_y, 0, zero_layer) - field_y)
    curl_y = forward(field_x, 0, zero_layer) - field_x - (forward(field_z, 1, row_rim[1]) - field_z)
    curl_z = forward(field_y, 1, row_rim[0]) - field_y - (forward(field_x, 2, col_rim[0]) - field_x)
    return jnp.stack([curl_x, curl_y, curl_z])

def curl_backward(magnetic, row_rim, col_rim):
    field_x, field_y, field_z = (magnetic[0], magnetic[1], magnetic[2])
    zero_layer = jnp.zeros(field_x.shape[1:], jnp.float32)
    curl_x = field_z - backward(field_z, 2, col_rim[1]) - (field_y - backward(field_y, 0, zero_layer))
    curl_y = field_x - backward(field_x, 0, zero_layer) - (field_z - backward(field_z, 1, row_rim[1]))
    curl_z = field_y - backward(field_y, 1, row_rim[0]) - (field_x - backward(field_x, 2, col_rim[0]))
    return jnp.stack([curl_x, curl_y, curl_z])

def reference(e_field, h_field, material, eps_table, src_pos, src_amp, freqs):
    update_scale = courant / eps_table[material]
    source_grid = jnp.zeros((LZ, NX, NY), jnp.float32).at[src_pos[:, 0], src_pos[:, 1], src_pos[:, 2]].add(src_amp)
    row_zero = jnp.zeros((2, LZ, NY), jnp.float32)
    col_zero = jnp.zeros((2, LZ, NX), jnp.float32)
    electric, magnetic = (e_field, h_field)
    real_sum = jnp.zeros((NF, 4, NX, NY), jnp.float32)
    imag_sum = jnp.zeros((NF, 4, NX, NY), jnp.float32)
    for step_index in range(STEPS):
        moment = float(step_index + 1)
        magnetic = magnetic - courant * curl_forward(electric, row_zero, col_zero)
        electric = electric + update_scale * curl_backward(magnetic, row_zero, col_zero)
        electric = electric.at[2].add(math.sin(source_rate * moment) * source_grid)
        face_now = jnp.stack([-magnetic[1, FACE], magnetic[0, FACE], electric[1, FACE], -electric[0, FACE]])
        real_sum = real_sum + face_now[None] * jnp.cos(freqs * moment)[:, None, None, None]
        imag_sum = imag_sum + face_now[None] * jnp.sin(freqs * moment)[:, None, None, None]
    currents = jnp.stack([real_sum.reshape(ITEMS, NX, NY), imag_sum.reshape(ITEMS, NX, NY)], 1).astype(jnp.bfloat16)
    u_index = jnp.arange(NA, dtype=jnp.int32)
    x_index = jnp.arange(NX, dtype=jnp.int32)
    y_index = jnp.arange(NY, dtype=jnp.int32)
    x_real, x_imag = chirp((u_index - NA // 2)[:, None], x_index[None, :], zoom_factor * NX)
    x_table = jnp.stack([x_real, x_imag]).astype(jnp.bfloat16).astype(jnp.float32)
    y_real, y_imag = chirp(y_index[:, None], (u_index + NA // 4)[None, :], zoom_factor * NY)
    y_table = jnp.concatenate([y_real, y_imag], 1).astype(jnp.bfloat16).astype(jnp.float32)
    inv_norm = 1.0 / math.sqrt(NX * NY)

    def one_item(item_currents):
        values = item_currents.astype(jnp.float32)
        product = jnp.einsum('aux,bxy->abuy', x_table, values, precision=lax.Precision.HIGHEST)
        sectioned = jnp.stack([product[0, 0] - product[1, 1], product[0, 1] + product[1, 0]]).astype(jnp.bfloat16)
        second = jnp.einsum('buy,yw->buw', sectioned.astype(jnp.float32), y_table, precision=lax.Precision.HIGHEST)
        result = jnp.stack([second[0, :, :NA] - second[1, :, NA:], second[0, :, NA:] + second[1, :, :NA]])
        return result * inv_norm
    far_all = lax.map(one_item, currents)
    far_field = jnp.transpose(far_all, (2, 0, 1, 3))
    return (electric, magnetic, far_field)
```

```python
import functools
import math

import jax
import jax.numpy as jnp
from jax import lax
from jax.experimental import pallas as pl
from jax.experimental.pallas import tpu as pltpu
from jax.sharding import PartitionSpec as P

LZ = 3
FACE = 1
STEPS = 2
NF = 2
NA = 1024
NMAT = 8

courant = 0.5
source_rate = 0.7
zoom_factor = 4

BASE = 32
CHUNK = 16
PAD = 128
ANY = pl.BlockSpec(memory_space=pl.ANY)
VM = pl.BlockSpec(memory_space=pltpu.VMEM)
SM = pl.BlockSpec(memory_space=pltpu.SMEM)
BIG = 60 * 1024 * 1024


def shifted(block, axis, distance):
    size = lax.axis_size(axis)
    route = [(i - distance, i) for i in range(size) if 0 <= i - distance < size]
    return lax.ppermute(block, axis, route)


def yee_kernel(
    grid_rows, grid_cols, parts,
    e_hbm, h_hbm, m_hbm, colf, colm, rowf, rowm, eps, pos, amp,
    e_out, h_out, sd_out,
    e_ext, h_ext, m_main, scale, src, first, sems,
):
    rows, cols = m_main.shape[1:]
    width = cols + PAD
    high = e_ext.shape[1]
    row0 = lax.axis_index("gx") * rows
    col0 = lax.axis_index("gy") * cols
    main_r = pl.ds(BASE, rows)
    copies = [
        pltpu.make_async_copy(e_hbm, e_ext.at[:, main_r, pl.ds(0, cols)], sems.at[0]),
        pltpu.make_async_copy(h_hbm, h_ext.at[:, main_r, pl.ds(0, cols)], sems.at[1]),
        pltpu.make_async_copy(m_hbm, m_main, sems.at[2]),
    ]
    for copy in copies:
        copy.start()
    count = amp.shape[1]
    step = min(count, 1024)
    used = high - 2 * CHUNK
    row_at = row0 + lax.broadcasted_iota(jnp.int32, (used, step), 0) + (CHUNK - BASE)
    lane = lax.broadcasted_iota(jnp.int32, (width, step), 0)
    col_at = col0 + jnp.where(lane < cols + PAD // 2, lane, lane - width)
    for start in range(0, count, step):
        at = pl.ds(start, step)
        amp_now = amp[:, at]
        hi = amp_now.astype(jnp.bfloat16).astype(jnp.float32)
        mid = (amp_now - hi).astype(jnp.bfloat16).astype(jnp.float32)
        low = amp_now - hi - mid
        hit_col = jnp.where(col_at == pos[2:3, at], 1.0, 0.0).astype(jnp.bfloat16)
        hit_row = row_at == pos[1:2, at]
        for layer in range(LZ):
            hit = hit_row & (pos[0:1, at] == layer)
            total = None
            for piece in (hi, mid, low):
                left = jnp.where(hit, piece, 0.0).astype(jnp.bfloat16)
                term = lax.dot_general(
                    left, hit_col, (((1,), (1,)), ((), ())), preferred_element_type=jnp.float32
                )
                total = term if total is None else total + term
            if start == 0:
                src[layer, CHUNK : CHUNK + used, :] = total
            else:
                src[layer, CHUNK : CHUNK + used, :] += total
    copies[2].wait()

    def scale_of(index, row, col):
        value = jnp.full(index.shape, eps[0], jnp.float32)
        for material in range(1, NMAT):
            value = jnp.where(index == material, eps[material], value)
        inside = (row >= 0) & (row < grid_rows) & (col >= 0) & (col < grid_cols)
        return jnp.where(inside, courant / value, 0.0)

    col_main = col0 + lax.broadcasted_iota(jnp.int32, (CHUNK, cols), 1)
    lane_pad = lax.broadcasted_iota(jnp.int32, (CHUNK, PAD), 1)
    col_pad = col0 + jnp.where(lane_pad < PAD // 2, cols + lane_pad, lane_pad - PAD)
    row_chunk = row0 + lax.broadcasted_iota(jnp.int32, (CHUNK, cols), 0)

    def fill(step_index, carry):
        r = pl.multiple_of(step_index * CHUNK, CHUNK)
        near = pl.ds(r, CHUNK)
        far = pl.ds(BASE + r, CHUNK)
        for layer in range(LZ):
            scale[layer, far, :cols] = scale_of(m_main[layer, near, :], row_chunk + r, col_main)
            scale[layer, far, cols:] = scale_of(
                colm[layer, near, :], row_chunk[:, :PAD] + r, col_pad
            )
        for plane in range(3 * LZ):
            e_ext[plane, far, cols:] = colf[plane, near, :]
            h_ext[plane, far, cols:] = colf[3 * LZ + plane, near, :]
        return carry

    lax.fori_loop(0, rows // CHUNK, fill, 0)
    lane_all = lax.broadcasted_iota(jnp.int32, (8, width), 1)
    col_all = col0 + jnp.where(lane_all < cols + PAD // 2, lane_all, lane_all - width)
    row_eight = row0 + lax.broadcasted_iota(jnp.int32, (8, width), 0)
    blank = jnp.zeros((8, width), jnp.float32)
    for place, target, offset, spare in (
        (0, BASE + rows, rows, BASE + rows + 8),
        (8, BASE - 8, -8, BASE - 16),
    ):
        for layer in range(LZ):
            scale[layer, target : target + 8, :] = scale_of(
                rowm[layer, place : place + 8, :], row_eight + offset, col_all
            )
            scale[layer, spare : spare + 8, :] = blank
        for plane in range(3 * LZ):
            e_ext[plane, target : target + 8, :] = rowf[plane, place : place + 8, :]
            h_ext[plane, target : target + 8, :] = rowf[3 * LZ + plane, place : place + 8, :]
            e_ext[plane, spare : spare + 8, :] = blank
            h_ext[plane, spare : spare + 8, :] = blank
    for plane in range(3 * LZ):
        e_ext[plane, high - 16 : high, :] = jnp.zeros((16, width), jnp.float32)
        h_ext[plane, 0:16, :] = jnp.zeros((16, width), jnp.float32)
    lane_c = lax.broadcasted_iota(jnp.int32, (CHUNK, width), 1)
    col_c = col0 + jnp.where(lane_c < cols + PAD // 2, lane_c, lane_c - width)
    weight = jnp.where(col_c >= 0, courant, 0.0)
    top = lax.axis_index("gx") == 0
    copies[0].wait()
    copies[1].wait()

    def magnetic_pass(index, carry):
        r = pl.multiple_of(index * CHUNK, CHUNK)
        now = pl.ds(r, CHUNK)
        more = pl.ds(r, CHUNK + 8)
        factor = weight * jnp.where(top & (index * CHUNK < BASE), 0.0, 1.0)
        zero = jnp.zeros((CHUNK, width), jnp.float32)
        ex = [e_ext[layer, now, :] for layer in range(LZ)] + [zero]
        ey = [e_ext[LZ + layer, now, :] for layer in range(LZ)] + [zero]
        for layer in range(LZ):
            ez = e_ext[2 * LZ + layer, now, :]
            ez_row = pltpu.roll(e_ext[2 * LZ + layer, more, :], CHUNK + 7, 0)[:CHUNK]
            ey_row = pltpu.roll(e_ext[LZ + layer, more, :], CHUNK + 7, 0)[:CHUNK]
            ez_col = pltpu.roll(ez, width - 1, 1)
            ex_col = pltpu.roll(ex[layer], width - 1, 1)
            curl_x = ez_col - ez - (ey[layer + 1] - ey[layer])
            curl_y = ex[layer + 1] - ex[layer] - (ez_row - ez)
            curl_z = ey_row - ey[layer] - (ex_col - ex[layer])
            for part, curl in enumerate((curl_x, curl_y, curl_z)):
                plane = part * LZ + layer
                h_ext[plane, now, :] = h_ext[plane, now, :] - factor * curl
        return carry

    def electric_pass(moment, last, index, carry):
        r = pl.multiple_of(index * CHUNK, CHUNK)
        now = pl.ds(r, CHUNK)
        more = pl.ds(pl.multiple_of(r - 8, 8), CHUNK + 8)
        drive = math.sin(source_rate * moment)
        zero = jnp.zeros((CHUNK, width), jnp.float32)
        hx = [zero] + [h_ext[layer, now, :] for layer in range(LZ)]
        hy = [zero] + [h_ext[LZ + layer, now, :] for layer in range(LZ)]
        for layer in range(LZ):
            hz = h_ext[2 * LZ + layer, now, :]
            hz_row = pltpu.roll(h_ext[2 * LZ + layer, more, :], 1, 0)[8:]
            hy_row = pltpu.roll(h_ext[LZ + layer, more, :], 1, 0)[8:]
            hx_now, hy_now = hx[layer + 1], hy[layer + 1]
            hz_col = pltpu.roll(hz, 1, 1)
            hx_col = pltpu.roll(hx_now, 1, 1)
            curl_x = hz - hz_col - (hy_now - hy[layer])
            curl_y = hx_now - hx[layer] - (hz - hz_row)
            curl_z = hy_now - hy_row - (hx_now - hx_col)
            factor = scale[layer, now, :]
            new_x = e_ext[layer, now, :] + factor * curl_x
            new_y = e_ext[LZ + layer, now, :] + factor * curl_y
            new_z = e_ext[2 * LZ + layer, now, :] + factor * curl_z + drive * src[layer, now, :]
            e_ext[layer, now, :] = new_x
            e_ext[LZ + layer, now, :] = new_y
            e_ext[2 * LZ + layer, now, :] = new_z
            if layer == FACE:
                faces = (-hy_now, hx_now, new_y, -new_x)
                for item, face in enumerate(faces):
                    if last:
                        old = first[item, now, :]
                        here = pl.ds(r - BASE, CHUNK)
                        span = cols // parts
                        for which, value in enumerate((old + face, face - old)):
                            value = value.astype(jnp.bfloat16)
                            for part in range(parts):
                                sd_out[item * parts + part, which, here, :] = value[
                                    :, part * span : (part + 1) * span
                                ]
                    else:
                        first[item, now, :] = face
        return carry

    chunks = high // CHUNK
    main0 = BASE // CHUNK
    main1 = main0 + rows // CHUNK
    lax.fori_loop(1, chunks - 1, magnetic_pass, 0)
    lax.fori_loop(1, chunks - 1, functools.partial(electric_pass, 1.0, False), 0)
    lax.fori_loop(1, main1, magnetic_pass, 0)
    out_h = pltpu.make_async_copy(h_ext.at[:, main_r, pl.ds(0, cols)], h_out, sems.at[3])
    out_h.start()
    lax.fori_loop(main0, main1, functools.partial(electric_pass, 2.0, True), 0)
    out_e = pltpu.make_async_copy(e_ext.at[:, main_r, pl.ds(0, cols)], e_out, sems.at[4])
    out_e.start()
    out_h.wait()
    out_e.wait()


def yee(e_field, h_field, material, eps_table, src_pos, src_amp):
    rows, cols = material.shape[1:]
    gx = lax.axis_size("gx")
    parts = gx // 4
    grid_rows = rows * gx
    grid_cols = cols * lax.axis_size("gy")
    planes = 3 * LZ
    e = e_field.reshape(planes, rows, cols)
    h = h_field.reshape(planes, rows, cols)
    mf = material.astype(jnp.float32)

    def edge(low, high, dim):
        cut = lambda a: lax.slice_in_dim(a, low, high, axis=dim)
        return jnp.concatenate([cut(e), cut(h), cut(mf)], 0)

    send_prev = jnp.swapaxes(edge(0, 2, 2), 1, 2)
    send_next = jnp.swapaxes(edge(cols - 2, cols, 2), 1, 2)
    right = shifted(send_prev, "gy", -1)
    left = shifted(send_next, "gy", 1)
    right = jnp.swapaxes(right, 1, 2)
    left = jnp.swapaxes(left, 1, 2)
    total = 2 * planes + LZ
    col_halo = jnp.concatenate(
        [right, jnp.zeros((total, rows, PAD - 4), jnp.float32), left], 2
    )
    send_up = jnp.concatenate([edge(0, 2, 1), col_halo[:, 0:2]], 2)
    send_down = jnp.concatenate([edge(rows - 2, rows, 1), col_halo[:, rows - 2 :]], 2)
    below = shifted(send_up, "gx", -1)
    above = shifted(send_down, "gx", 1)
    row_halo = jnp.concatenate(
        [below, jnp.zeros((total, 12, cols + PAD), jnp.float32), above], 1
    )
    colf, colm = col_halo[: 2 * planes], col_halo[2 * planes :].astype(jnp.int32)
    rowf, rowm = row_halo[: 2 * planes], row_halo[2 * planes :].astype(jnp.int32)
    high = rows + 2 * BASE
    width = cols + PAD
    f32 = jnp.float32
    out = pl.pallas_call(
        functools.partial(yee_kernel, grid_rows, grid_cols, parts),
        out_shape=(
            jax.ShapeDtypeStruct((planes, rows, cols), f32),
            jax.ShapeDtypeStruct((planes, rows, cols), f32),
            jax.ShapeDtypeStruct((gx, 2, rows, cols // parts), jnp.bfloat16),
        ),
        in_specs=[ANY, ANY, ANY, VM, VM, VM, VM, SM, VM, VM],
        out_specs=(ANY, ANY, VM),
        scratch_shapes=[
            pltpu.VMEM((planes, high, width), f32),
            pltpu.VMEM((planes, high, width), f32),
            pltpu.VMEM((LZ, rows, cols), jnp.int32),
            pltpu.VMEM((LZ, high, width), f32),
            pltpu.VMEM((LZ, high, width), f32),
            pltpu.VMEM((4, high, width), f32),
            pltpu.SemaphoreType.DMA((5,)),
        ],
        compiler_params=pltpu.CompilerParams(vmem_limit_bytes=BIG),
        name="yee",
    )(
        e, h, material, colf, colm, rowf, rowm,
        eps_table, jnp.swapaxes(src_pos, 0, 1), src_amp[None, :],
    )
    return out


def table_kernel(a_re, a_im, b_re, b_im, out):
    lo_re, lo_im = b_re[...], b_im[...]
    for block in range(a_re.shape[1]):
        hi_re = a_re[:, block : block + 1]
        hi_im = a_im[:, block : block + 1]
        at = slice(block * 128, block * 128 + 128)
        out[0, 0, :, at] = (hi_re * lo_re - hi_im * lo_im).astype(jnp.bfloat16)
        out[0, 1, :, at] = (hi_re * lo_im + hi_im * lo_re).astype(jnp.bfloat16)


def unit(phase, period):
    angle = jnp.remainder(phase, period).astype(jnp.float32) * (2.0 * math.pi / period)
    return jnp.cos(angle), -jnp.sin(angle)


def table(row_index, first, length, period, blocks):
    count = row_index.shape[0]
    high = first + 128 * jnp.arange(length // 128, dtype=jnp.int32)
    low = jnp.arange(128, dtype=jnp.int32)
    a_re, a_im = unit(row_index[:, None] * high[None, :], period)
    b_re, b_im = unit(row_index[:, None] * low[None, :], period)
    size = count // blocks
    one = pl.BlockSpec((size, length // 128), lambda i: (i, 0))
    two = pl.BlockSpec((size, 128), lambda i: (i, 0))
    return pl.pallas_call(
        table_kernel,
        grid=(blocks,),
        out_shape=jax.ShapeDtypeStruct((blocks, 2, size, length), jnp.bfloat16),
        in_specs=[one, one, two, two],
        out_specs=pl.BlockSpec((1, 2, size, length), lambda i: (i, 0, 0, 0)),
        cost_estimate=pl.CostEstimate(
            flops=8 * count * length, bytes_accessed=4 * count * length, transcendentals=0
        ),
        name="chirp",
    )(a_re, a_im, b_re, b_im)


def rows_kernel(mix, tab, v, out):
    nu = tab.shape[2]
    span = v.shape[3]
    left = tab[0].reshape(2 * nu, tab.shape[3])
    got = []
    for which in range(2):
        right = v[:, which].reshape(-1, span)
        both = jnp.dot(left, right, preferred_element_type=jnp.float32)
        got.append((both[:nu], both[nu:]))
    (s_re, s_im), (d_re, d_im) = got
    for f in range(NF):
        p_re, p_im, q_re, q_im = (mix[f, i] for i in range(4))
        re = p_re * s_re - p_im * s_im + (q_re * d_re - q_im * d_im)
        im = p_re * s_im + p_im * s_re + (q_re * d_im + q_im * d_re)
        out[0, f, 0] = re.astype(jnp.bfloat16)
        out[0, f, 1] = im.astype(jnp.bfloat16)


def cols_kernel(g, tab, out):
    parts, span = g.shape[1], g.shape[5]
    width = tab.shape[2]
    shares = out.shape[0]
    vb = out.shape[4]
    y_re = tab[0, 0]
    y_im = tab[0, 1]
    g_re = jnp.concatenate([g[0, p, 0, 0] for p in range(parts)], 1)
    g_im = jnp.concatenate([g[0, p, 0, 1] for p in range(parts)], 1)
    dot = functools.partial(jnp.dot, preferred_element_type=jnp.float32)
    re = dot(g_re, y_re) - dot(g_im, y_im)
    im = dot(g_re, y_im) + dot(g_im, y_re)
    for share in range(shares):
        out[share, 0, 0] = re[:, share * vb : (share + 1) * vb].astype(out.dtype)
        out[share, 0, 1] = im[:, share * vb : (share + 1) * vb].astype(out.dtype)


def on_device(e_field, h_field, material, eps_table, src_pos, src_amp, freqs):
    rows, cols = material.shape[1:]
    gx, gy = lax.axis_size("gx"), lax.axis_size("gy")
    grid_rows, grid_cols = rows * gx, cols * gy
    parts = gx // 4
    span = cols // parts
    nu = NA // gx
    vb = NA // gy
    col_start = lax.axis_index("gy") * cols
    bf16 = jnp.bfloat16
    angle_index = jnp.arange(NA, dtype=jnp.int32)
    x_tab = table(angle_index - NA // 2, 0, grid_rows, zoom_factor * grid_rows, gx)
    y_cells = col_start + jnp.arange(cols, dtype=jnp.int32)
    y_tab = table(y_cells, NA // 4, NA, zoom_factor * grid_cols, 1)
    e_new, h_new, sd = yee(e_field, h_field, material, eps_table, src_pos, src_amp)
    got = lax.all_to_all(sd, "gx", split_axis=0, concat_axis=0, tiled=True)
    turn_re, turn_im = jnp.cos(1.5 * freqs), jnp.sin(1.5 * freqs)
    half_re, half_im = jnp.cos(0.5 * freqs), jnp.sin(0.5 * freqs)
    mix = jnp.stack(
        [turn_re * half_re, turn_im * half_re, -turn_im * half_im, turn_re * half_im], 1
    )
    g = pl.pallas_call(
        rows_kernel,
        grid=(gx,),
        out_shape=jax.ShapeDtypeStruct((gx, NF, 2, nu, span), bf16),
        in_specs=[
            SM,
            pl.BlockSpec((1, 2, nu, grid_rows), lambda i: (i, 0, 0, 0)),
            pl.BlockSpec((gx, 2, rows, span), lambda i: (0, 0, 0, 0)),
        ],
        out_specs=pl.BlockSpec((1, NF, 2, nu, span), lambda i: (i, 0, 0, 0, 0)),
        compiler_params=pltpu.CompilerParams(vmem_limit_bytes=BIG),
        name="rows",
    )(mix, x_tab, got)
    moved = lax.all_to_all(g, "gx", split_axis=0, concat_axis=0, tiled=True)
    moved = moved.reshape(4, parts, NF, 2, nu, span)
    share = pl.pallas_call(
        cols_kernel,
        grid=(NF, 4),
        out_shape=jax.ShapeDtypeStruct((gy, NF * 4, 2, nu, vb), bf16),
        in_specs=[
            pl.BlockSpec((1, parts, 1, 2, nu, span), lambda f, k: (k, 0, f, 0, 0, 0)),
            pl.BlockSpec((1, 2, cols, NA), lambda f, k: (0, 0, 0, 0)),
        ],
        out_specs=pl.BlockSpec((gy, 1, 2, nu, vb), lambda f, k: (0, f * 4 + k, 0, 0, 0)),
        compiler_params=pltpu.CompilerParams(vmem_limit_bytes=BIG),
        name="cols",
    )(moved, y_tab)
    inv_norm = 1.0 / math.sqrt(grid_rows * grid_cols)
    summed = lax.psum_scatter(share, "gy", scatter_dimension=0, tiled=True)
    far = jnp.transpose(summed[0].astype(jnp.float32) * inv_norm, (2, 0, 1, 3))
    shape = e_field.shape
    return (e_new.reshape(shape), h_new.reshape(shape), far)


def solution(mesh):
    placed = (
        P(None, None, "gx", "gy"),
        P(None, None, "gx", "gy"),
        P(None, "gx", "gy"),
        P(),
        P(),
        P(),
        P(),
    )
    return jax.shard_map(
        on_device,
        mesh=mesh,
        in_specs=placed,
        out_specs=(P(None, None, "gx", "gy"), P(None, None, "gx", "gy"), P("gx", None, None, "gy")),
        check_vma=False,
    )
```

```python
import functools
import math

import jax
import jax.numpy as jnp
from jax import lax
from jax.experimental import pallas as pl
from jax.experimental.pallas import tpu as pltpu
from jax.sharding import PartitionSpec as P

LZ = 3
FACE = 1
STEPS = 2
NF = 2
NA = 1024
NMAT = 8

courant = 0.5
source_rate = 0.7
zoom_factor = 4

BASE = 32
CHUNK = 16
PAD = 128
ANY = pl.BlockSpec(memory_space=pl.ANY)
VM = pl.BlockSpec(memory_space=pltpu.VMEM)
SM = pl.BlockSpec(memory_space=pltpu.SMEM)
BIG = 60 * 1024 * 1024


def shifted(block, axis, distance):
    size = lax.axis_size(axis)
    route = [(i - distance, i) for i in range(size) if 0 <= i - distance < size]
    return lax.ppermute(block, axis, route)


def yee_kernel(
    grid_rows, grid_cols, parts,
    e_hbm, h_hbm, m_hbm, colh, rowh, eps, pos, amp,
    e_out, h_out, sd_out,
    e_ext, h_ext, m_main, scale, src, first, sems,
):
    rows, cols = m_main.shape[1:]
    width = cols + PAD
    high = e_ext.shape[1]
    row0 = lax.axis_index("gx") * rows
    col0 = lax.axis_index("gy") * cols
    main_r = pl.ds(BASE, rows)
    copies = [
        pltpu.make_async_copy(e_hbm, e_ext.at[:, main_r, pl.ds(0, cols)], sems.at[0]),
        pltpu.make_async_copy(h_hbm, h_ext.at[:, main_r, pl.ds(0, cols)], sems.at[1]),
        pltpu.make_async_copy(m_hbm, m_main, sems.at[2]),
    ]
    for copy in copies:
        copy.start()
    count = amp.shape[1]
    step = min(count, 1024)
    used = high - 2 * CHUNK
    row_at = row0 + lax.broadcasted_iota(jnp.int32, (used, step), 0) + (CHUNK - BASE)
    lane = lax.broadcasted_iota(jnp.int32, (width, step), 0)
    col_at = col0 + jnp.where(lane < cols + PAD // 2, lane, lane - width)
    for start in range(0, count, step):
        at = pl.ds(start, step)
        amp_now = amp[:, at]
        hi = amp_now.astype(jnp.bfloat16).astype(jnp.float32)
        mid = (amp_now - hi).astype(jnp.bfloat16).astype(jnp.float32)
        low = amp_now - hi - mid
        hit_col = jnp.where(col_at == pos[2:3, at], 1.0, 0.0).astype(jnp.bfloat16)
        hit_row = row_at == pos[1:2, at]
        for layer in range(LZ):
            hit = hit_row & (pos[0:1, at] == layer)
            total = None
            for piece in (hi, mid, low):
                left = jnp.where(hit, piece, 0.0).astype(jnp.bfloat16)
                term = lax.dot_general(
                    left, hit_col, (((1,), (1,)), ((), ())), preferred_element_type=jnp.float32
                )
                total = term if total is None else total + term
            if start == 0:
                src[layer, CHUNK : CHUNK + used, :] = total
            else:
                src[layer, CHUNK : CHUNK + used, :] += total
    copies[2].wait()

    def scale_of(index, row, col):
        value = jnp.full(index.shape, eps[0], jnp.float32)
        for material in range(1, NMAT):
            value = jnp.where(index == material, eps[material], value)
        inside = (row >= 0) & (row < grid_rows) & (col >= 0) & (col < grid_cols)
        return jnp.where(inside, courant / value, 0.0)

    col_main = col0 + lax.broadcasted_iota(jnp.int32, (CHUNK, cols), 1)
    lane_pad = lax.broadcasted_iota(jnp.int32, (CHUNK, PAD), 1)
    col_pad = col0 + jnp.where(lane_pad < PAD // 2, cols + lane_pad, lane_pad - PAD)
    row_chunk = row0 + lax.broadcasted_iota(jnp.int32, (CHUNK, cols), 0)

    def fill(step_index, carry):
        r = pl.multiple_of(step_index * CHUNK, CHUNK)
        near = pl.ds(r, CHUNK)
        far = pl.ds(BASE + r, CHUNK)
        for layer in range(LZ):
            scale[layer, far, :cols] = scale_of(m_main[layer, near, :], row_chunk + r, col_main)
            scale[layer, far, cols:] = scale_of(
                colh[6 * LZ + layer, near, :], row_chunk[:, :PAD] + r, col_pad
            )
        for plane in range(3 * LZ):
            e_ext[plane, far, cols:] = colh[plane, near, :]
            h_ext[plane, far, cols:] = colh[3 * LZ + plane, near, :]
        return carry

    lax.fori_loop(0, rows // CHUNK, fill, 0)
    lane_all = lax.broadcasted_iota(jnp.int32, (8, width), 1)
    col_all = col0 + jnp.where(lane_all < cols + PAD // 2, lane_all, lane_all - width)
    row_eight = row0 + lax.broadcasted_iota(jnp.int32, (8, width), 0)
    blank = jnp.zeros((8, width), jnp.float32)
    for place, target, offset, spare in (
        (0, BASE + rows, rows, BASE + rows + 8),
        (8, BASE - 8, -8, BASE - 16),
    ):
        for layer in range(LZ):
            scale[layer, target : target + 8, :] = scale_of(
                rowh[6 * LZ + layer, place : place + 8, :], row_eight + offset, col_all
            )
            scale[layer, spare : spare + 8, :] = blank
        for plane in range(3 * LZ):
            e_ext[plane, target : target + 8, :] = rowh[plane, place : place + 8, :]
            h_ext[plane, target : target + 8, :] = rowh[3 * LZ + plane, place : place + 8, :]
            e_ext[plane, spare : spare + 8, :] = blank
            h_ext[plane, spare : spare + 8, :] = blank
    for plane in range(3 * LZ):
        e_ext[plane, high - 16 : high, :] = jnp.zeros((16, width), jnp.float32)
        h_ext[plane, 0:16, :] = jnp.zeros((16, width), jnp.float32)
    lane_c = lax.broadcasted_iota(jnp.int32, (CHUNK, width), 1)
    col_c = col0 + jnp.where(lane_c < cols + PAD // 2, lane_c, lane_c - width)
    weight = jnp.where(col_c >= 0, courant, 0.0)
    top = lax.axis_index("gx") == 0
    copies[0].wait()
    copies[1].wait()

    def magnetic_pass(index, carry):
        r = pl.multiple_of(index * CHUNK, CHUNK)
        now = pl.ds(r, CHUNK)
        more = pl.ds(r, CHUNK + 8)
        factor = weight * jnp.where(top & (index * CHUNK < BASE), 0.0, 1.0)
        zero = jnp.zeros((CHUNK, width), jnp.float32)
        ex = [e_ext[layer, now, :] for layer in range(LZ)] + [zero]
        ey = [e_ext[LZ + layer, now, :] for layer in range(LZ)] + [zero]
        for layer in range(LZ):
            ez = e_ext[2 * LZ + layer, now, :]
            ez_row = pltpu.roll(e_ext[2 * LZ + layer, more, :], CHUNK + 7, 0)[:CHUNK]
            ey_row = pltpu.roll(e_ext[LZ + layer, more, :], CHUNK + 7, 0)[:CHUNK]
            ez_col = pltpu.roll(ez, width - 1, 1)
            ex_col = pltpu.roll(ex[layer], width - 1, 1)
            curl_x = ez_col - ez - (ey[layer + 1] - ey[layer])
            curl_y = ex[layer + 1] - ex[layer] - (ez_row - ez)
            curl_z = ey_row - ey[layer] - (ex_col - ex[layer])
            for part, curl in enumerate((curl_x, curl_y, curl_z)):
                plane = part * LZ + layer
                h_ext[plane, now, :] = h_ext[plane, now, :] - factor * curl
        return carry

    def electric_pass(moment, last, index, carry):
        r = pl.multiple_of(index * CHUNK, CHUNK)
        now = pl.ds(r, CHUNK)
        more = pl.ds(pl.multiple_of(r - 8, 8), CHUNK + 8)
        drive = math.sin(source_rate * moment)
        zero = jnp.zeros((CHUNK, width), jnp.float32)
        hx = [zero] + [h_ext[layer, now, :] for layer in range(LZ)]
        hy = [zero] + [h_ext[LZ + layer, now, :] for layer in range(LZ)]
        for layer in range(LZ):
            hz = h_ext[2 * LZ + layer, now, :]
            hz_row = pltpu.roll(h_ext[2 * LZ + layer, more, :], 1, 0)[8:]
            hy_row = pltpu.roll(h_ext[LZ + layer, more, :], 1, 0)[8:]
            hx_now, hy_now = hx[layer + 1], hy[layer + 1]
            hz_col = pltpu.roll(hz, 1, 1)
            hx_col = pltpu.roll(hx_now, 1, 1)
            curl_x = hz - hz_col - (hy_now - hy[layer])
            curl_y = hx_now - hx[layer] - (hz - hz_row)
            curl_z = hy_now - hy_row - (hx_now - hx_col)
            factor = scale[layer, now, :]
            new_x = e_ext[layer, now, :] + factor * curl_x
            new_y = e_ext[LZ + layer, now, :] + factor * curl_y
            new_z = e_ext[2 * LZ + layer, now, :] + factor * curl_z + drive * src[layer, now, :]
            e_ext[layer, now, :] = new_x
            e_ext[LZ + layer, now, :] = new_y
            e_ext[2 * LZ + layer, now, :] = new_z
            if layer == FACE:
                faces = (-hy_now, hx_now, new_y, -new_x)
                for item, face in enumerate(faces):
                    if last:
                        old = first[item, now, :]
                        here = pl.ds(r - BASE, CHUNK)
                        span = cols // parts
                        for which, value in enumerate((old + face, face - old)):
                            value = value.astype(jnp.bfloat16)
                            for part in range(parts):
                                sd_out[item * parts + part, which, here, :] = value[
                                    :, part * span : (part + 1) * span
                                ]
                    else:
                        first[item, now, :] = face
        return carry

    chunks = high // CHUNK
    main0 = BASE // CHUNK
    main1 = main0 + rows // CHUNK
    lax.fori_loop(1, chunks - 1, magnetic_pass, 0)
    lax.fori_loop(1, chunks - 1, functools.partial(electric_pass, 1.0, False), 0)
    lax.fori_loop(1, main1, magnetic_pass, 0)
    out_h = pltpu.make_async_copy(h_ext.at[:, main_r, pl.ds(0, cols)], h_out, sems.at[3])
    out_h.start()
    lax.fori_loop(main0, main1, functools.partial(electric_pass, 2.0, True), 0)
    out_e = pltpu.make_async_copy(e_ext.at[:, main_r, pl.ds(0, cols)], e_out, sems.at[4])
    out_e.start()
    out_h.wait()
    out_e.wait()


def yee(e_field, h_field, material, eps_table, src_pos, src_amp):
    rows, cols = material.shape[1:]
    gx = lax.axis_size("gx")
    parts = gx // 4
    grid_rows = rows * gx
    grid_cols = cols * lax.axis_size("gy")
    planes = 3 * LZ
    e = e_field.reshape(planes, rows, cols)
    h = h_field.reshape(planes, rows, cols)

    def edge(low, high, dim):
        cut = lambda a: lax.slice_in_dim(a, low, high, axis=dim)
        return jnp.concatenate([cut(e), cut(h), cut(material).astype(jnp.float32)], 0)

    send_prev = jnp.swapaxes(edge(0, 2, 2), 1, 2)
    send_next = jnp.swapaxes(edge(cols - 2, cols, 2), 1, 2)
    right = shifted(send_prev, "gy", -1)
    left = shifted(send_next, "gy", 1)
    right = jnp.swapaxes(right, 1, 2)
    left = jnp.swapaxes(left, 1, 2)
    total = 2 * planes + LZ
    col_halo = jnp.concatenate(
        [right, jnp.zeros((total, rows, PAD - 4), jnp.float32), left], 2
    )
    send_up = jnp.concatenate([edge(0, 2, 1), col_halo[:, 0:2]], 2)
    send_down = jnp.concatenate([edge(rows - 2, rows, 1), col_halo[:, rows - 2 :]], 2)
    below = shifted(send_up, "gx", -1)
    above = shifted(send_down, "gx", 1)
    row_halo = jnp.concatenate(
        [below, jnp.zeros((total, 12, cols + PAD), jnp.float32), above], 1
    )
    high = rows + 2 * BASE
    width = cols + PAD
    f32 = jnp.float32
    out = pl.pallas_call(
        functools.partial(yee_kernel, grid_rows, grid_cols, parts),
        out_shape=(
            jax.ShapeDtypeStruct((planes, rows, cols), f32),
            jax.ShapeDtypeStruct((planes, rows, cols), f32),
            jax.ShapeDtypeStruct((gx, 2, rows, cols // parts), jnp.bfloat16),
        ),
        in_specs=[ANY, ANY, ANY, VM, VM, SM, VM, VM],
        out_specs=(ANY, ANY, VM),
        scratch_shapes=[
            pltpu.VMEM((planes, high, width), f32),
            pltpu.VMEM((planes, high, width), f32),
            pltpu.VMEM((LZ, rows, cols), jnp.int32),
            pltpu.VMEM((LZ, high, width), f32),
            pltpu.VMEM((LZ, high, width), f32),
            pltpu.VMEM((4, high, width), f32),
            pltpu.SemaphoreType.DMA((5,)),
        ],
        compiler_params=pltpu.CompilerParams(vmem_limit_bytes=BIG),
        name="yee",
    )(
        e, h, material, col_halo, row_halo,
        eps_table, jnp.swapaxes(src_pos, 0, 1), src_amp[None, :],
    )
    return out


def table_kernel(a_re, a_im, b_re, b_im, out):
    lo_re, lo_im = b_re[...], b_im[...]
    for block in range(a_re.shape[1]):
        hi_re = a_re[:, block : block + 1]
        hi_im = a_im[:, block : block + 1]
        at = slice(block * 128, block * 128 + 128)
        out[0, 0, :, at] = (hi_re * lo_re - hi_im * lo_im).astype(jnp.bfloat16)
        out[0, 1, :, at] = (hi_re * lo_im + hi_im * lo_re).astype(jnp.bfloat16)


def unit(phase, period):
    angle = jnp.remainder(phase, period).astype(jnp.float32) * (2.0 * math.pi / period)
    return jnp.cos(angle), -jnp.sin(angle)


def table(row_index, first, length, period, blocks):
    count = row_index.shape[0]
    high = first + 128 * jnp.arange(length // 128, dtype=jnp.int32)
    low = jnp.arange(128, dtype=jnp.int32)
    a_re, a_im = unit(row_index[:, None] * high[None, :], period)
    b_re, b_im = unit(row_index[:, None] * low[None, :], period)
    size = count // blocks
    one = pl.BlockSpec((size, length // 128), lambda i: (i, 0))
    two = pl.BlockSpec((size, 128), lambda i: (i, 0))
    return pl.pallas_call(
        table_kernel,
        grid=(blocks,),
        out_shape=jax.ShapeDtypeStruct((blocks, 2, size, length), jnp.bfloat16),
        in_specs=[one, one, two, two],
        out_specs=pl.BlockSpec((1, 2, size, length), lambda i: (i, 0, 0, 0)),
        cost_estimate=pl.CostEstimate(
            flops=8 * count * length, bytes_accessed=4 * count * length, transcendentals=0
        ),
        name="chirp",
    )(a_re, a_im, b_re, b_im)


def rows_kernel(mix, tab, v, *outs):
    group, _, nu, depth = tab.shape
    span = v.shape[3]
    left = tab[...].reshape(group * 2 * nu, depth)
    got = []
    for which in range(2):
        right = v[:, which].reshape(-1, span)
        both = jnp.dot(left, right, preferred_element_type=jnp.float32)
        got.append(both.reshape(group, 2, nu, span))
    for f in range(NF):
        p_re, p_im, q_re, q_im = (mix[f, i] for i in range(4))
        for b in range(group):
            s_re, s_im = got[0][b, 0], got[0][b, 1]
            d_re, d_im = got[1][b, 0], got[1][b, 1]
            re = p_re * s_re - p_im * s_im + (q_re * d_re - q_im * d_im)
            im = p_re * s_im + p_im * s_re + (q_re * d_im + q_im * d_re)
            outs[f][b, 0] = re.astype(jnp.bfloat16)
            outs[f][b, 1] = im.astype(jnp.bfloat16)


def cols_kernel(g, tab, out, left):
    parts, nu, span = g.shape[1], g.shape[3], g.shape[4]

    @pl.when(pl.program_id(0) == 0)
    def _():
        for k in range(4):
            for part in range(parts):
                for c in range(2):
                    left[c, k * nu : (k + 1) * nu, part * span : (part + 1) * span] = g[
                        k, part, c
                    ]

    y_re = tab[0, 0]
    y_im = tab[0, 1]
    dot = functools.partial(jnp.dot, preferred_element_type=jnp.float32)
    re = dot(left[0], y_re) - dot(left[1], y_im)
    im = dot(left[0], y_im) + dot(left[1], y_re)
    for k in range(4):
        out[0, k, 0] = re[k * nu : (k + 1) * nu].astype(out.dtype)
        out[0, k, 1] = im[k * nu : (k + 1) * nu].astype(out.dtype)


def on_device(e_field, h_field, material, eps_table, src_pos, src_amp, freqs):
    rows, cols = material.shape[1:]
    gx, gy = lax.axis_size("gx"), lax.axis_size("gy")
    grid_rows, grid_cols = rows * gx, cols * gy
    parts = gx // 4
    span = cols // parts
    nu = NA // gx
    vb = NA // gy
    col_start = lax.axis_index("gy") * cols
    bf16 = jnp.bfloat16
    angle_index = jnp.arange(NA, dtype=jnp.int32)
    x_tab = table(angle_index - NA // 2, 0, grid_rows, zoom_factor * grid_rows, gx)
    y_cells = col_start + jnp.arange(cols, dtype=jnp.int32)
    y_tab = table(y_cells, NA // 4, NA, zoom_factor * grid_cols, 1)
    e_new, h_new, sd = yee(e_field, h_field, material, eps_table, src_pos, src_amp)
    got = lax.all_to_all(sd, "gx", split_axis=0, concat_axis=0, tiled=True)
    turn_re, turn_im = jnp.cos(1.5 * freqs), jnp.sin(1.5 * freqs)
    half_re, half_im = jnp.cos(0.5 * freqs), jnp.sin(0.5 * freqs)
    mix = jnp.stack(
        [turn_re * half_re, turn_im * half_re, -turn_im * half_im, turn_re * half_im], 1
    )
    group = 2
    halves = pl.pallas_call(
        rows_kernel,
        grid=(gx // group,),
        out_shape=[jax.ShapeDtypeStruct((gx, 2, nu, span), bf16)] * NF,
        in_specs=[
            SM,
            pl.BlockSpec((group, 2, nu, grid_rows), lambda i: (i, 0, 0, 0)),
            pl.BlockSpec((gx, 2, rows, span), lambda i: (0, 0, 0, 0)),
        ],
        out_specs=[pl.BlockSpec((group, 2, nu, span), lambda i: (i, 0, 0, 0))] * NF,
        compiler_params=pltpu.CompilerParams(vmem_limit_bytes=BIG),
        name="rows",
    )(mix, x_tab, got)
    inv_norm = 1.0 / math.sqrt(grid_rows * grid_cols)
    fars = []
    for g in halves:
        moved = lax.all_to_all(g, "gx", split_axis=0, concat_axis=0, tiled=True)
        moved = moved.reshape(4, parts, 2, nu, span)
        share = pl.pallas_call(
            cols_kernel,
            grid=(gy,),
            out_shape=jax.ShapeDtypeStruct((gy, 4, 2, nu, vb), bf16),
            in_specs=[
                pl.BlockSpec((4, parts, 2, nu, span), lambda j: (0, 0, 0, 0, 0)),
                pl.BlockSpec((1, 2, cols, vb), lambda j: (0, 0, 0, j)),
            ],
            out_specs=pl.BlockSpec((1, 4, 2, nu, vb), lambda j: (j, 0, 0, 0, 0)),
            scratch_shapes=[pltpu.VMEM((2, 4 * nu, cols), bf16)],
            compiler_params=pltpu.CompilerParams(vmem_limit_bytes=BIG),
            cost_estimate=pl.CostEstimate(
                flops=64 * nu * cols * NA, bytes_accessed=16 * nu * NA, transcendentals=0
            ),
            name="cols",
        )(moved, y_tab)
        summed = lax.psum_scatter(share, "gy", scatter_dimension=0, tiled=True)
        fars.append(jnp.transpose(summed[0].astype(jnp.float32) * inv_norm, (2, 0, 1, 3)))
    far = jnp.concatenate(fars, 1)
    shape = e_field.shape
    return (e_new.reshape(shape), h_new.reshape(shape), far)


def solution(mesh):
    placed = (
        P(None, None, "gx", "gy"),
        P(None, None, "gx", "gy"),
        P(None, "gx", "gy"),
        P(),
        P(),
        P(),
        P(),
    )
    return jax.shard_map(
        on_device,
        mesh=mesh,
        in_specs=placed,
        out_specs=(P(None, None, "gx", "gy"), P(None, None, "gx", "gy"), P("gx", None, None, "gy")),
        check_vma=False,
    )
```

```python
import functools
import math

import jax
import jax.numpy as jnp
from jax import lax
from jax.experimental import pallas as pl
from jax.experimental.pallas import tpu as pltpu
from jax.sharding import PartitionSpec as P

LZ = 3
FACE = 1
STEPS = 2
NF = 2
NA = 1024
NMAT = 8

courant = 0.5
source_rate = 0.7
zoom_factor = 4

BASE = 32
CHUNK = 16
SETS = 2
EACH = 4 // SETS
PAD = 128
ANY = pl.BlockSpec(memory_space=pl.ANY)
VM = pl.BlockSpec(memory_space=pltpu.VMEM)
SM = pl.BlockSpec(memory_space=pltpu.SMEM)
BIG = 60 * 1024 * 1024


def shifted(block, axis, distance):
    size = lax.axis_size(axis)
    route = [(i - distance, i) for i in range(size) if 0 <= i - distance < size]
    return lax.ppermute(block, axis, route)


def yee_kernel(
    grid_rows, grid_cols, gx,
    e_hbm, h_hbm, m_hbm, colh, rowh, eps, pos, amp,
    e_out, h_out, *rest,
):
    sd_outs, (e_ext, h_ext, m_main, scale, src, first, sems) = rest[:SETS], rest[SETS:]
    rows, cols = m_main.shape[1:]
    width = cols + PAD
    high = e_ext.shape[1]
    row0 = lax.axis_index("gx") * rows
    col0 = lax.axis_index("gy") * cols
    main_r = pl.ds(BASE, rows)
    copies = [
        pltpu.make_async_copy(e_hbm, e_ext.at[:, main_r, pl.ds(0, cols)], sems.at[0]),
        pltpu.make_async_copy(h_hbm, h_ext.at[:, main_r, pl.ds(0, cols)], sems.at[1]),
        pltpu.make_async_copy(m_hbm, m_main, sems.at[2]),
    ]
    for copy in copies:
        copy.start()
    count = amp.shape[1]
    step = min(count, 1024)
    used = high - 2 * CHUNK
    row_at = row0 + lax.broadcasted_iota(jnp.int32, (used, step), 0) + (CHUNK - BASE)
    lane = lax.broadcasted_iota(jnp.int32, (width, step), 0)
    col_at = col0 + jnp.where(lane < cols + PAD // 2, lane, lane - width)
    for start in range(0, count, step):
        at = pl.ds(start, step)
        amp_now = amp[:, at]
        hi = amp_now.astype(jnp.bfloat16).astype(jnp.float32)
        mid = (amp_now - hi).astype(jnp.bfloat16).astype(jnp.float32)
        low = amp_now - hi - mid
        hit_col = jnp.where(col_at == pos[2:3, at], 1.0, 0.0).astype(jnp.bfloat16)
        hit_row = row_at == pos[1:2, at]
        for layer in range(LZ):
            hit = hit_row & (pos[0:1, at] == layer)
            total = None
            for piece in (hi, mid, low):
                left = jnp.where(hit, piece, 0.0).astype(jnp.bfloat16)
                term = lax.dot_general(
                    left, hit_col, (((1,), (1,)), ((), ())), preferred_element_type=jnp.float32
                )
                total = term if total is None else total + term
            if start == 0:
                src[layer, CHUNK : CHUNK + used, :] = total
            else:
                src[layer, CHUNK : CHUNK + used, :] += total
    copies[2].wait()

    def scale_of(index, row, col):
        value = jnp.full(index.shape, eps[0], jnp.float32)
        for material in range(1, NMAT):
            value = jnp.where(index == material, eps[material], value)
        inside = (row >= 0) & (row < grid_rows) & (col >= 0) & (col < grid_cols)
        return jnp.where(inside, courant / value, 0.0)

    col_main = col0 + lax.broadcasted_iota(jnp.int32, (CHUNK, cols), 1)
    lane_pad = lax.broadcasted_iota(jnp.int32, (CHUNK, PAD), 1)
    col_pad = col0 + jnp.where(lane_pad < PAD // 2, cols + lane_pad, lane_pad - PAD)
    row_chunk = row0 + lax.broadcasted_iota(jnp.int32, (CHUNK, cols), 0)

    def fill(step_index, carry):
        r = pl.multiple_of(step_index * CHUNK, CHUNK)
        near = pl.ds(r, CHUNK)
        far = pl.ds(BASE + r, CHUNK)
        for layer in range(LZ):
            scale[layer, far, :cols] = scale_of(m_main[layer, near, :], row_chunk + r, col_main)
            scale[layer, far, cols:] = scale_of(
                colh[6 * LZ + layer, near, :], row_chunk[:, :PAD] + r, col_pad
            )
        for plane in range(3 * LZ):
            e_ext[plane, far, cols:] = colh[plane, near, :]
            h_ext[plane, far, cols:] = colh[3 * LZ + plane, near, :]
        return carry

    lax.fori_loop(0, rows // CHUNK, fill, 0)
    lane_all = lax.broadcasted_iota(jnp.int32, (8, width), 1)
    col_all = col0 + jnp.where(lane_all < cols + PAD // 2, lane_all, lane_all - width)
    row_eight = row0 + lax.broadcasted_iota(jnp.int32, (8, width), 0)
    blank = jnp.zeros((8, width), jnp.float32)
    for place, target, offset, spare in (
        (0, BASE + rows, rows, BASE + rows + 8),
        (8, BASE - 8, -8, BASE - 16),
    ):
        for layer in range(LZ):
            scale[layer, target : target + 8, :] = scale_of(
                rowh[6 * LZ + layer, place : place + 8, :], row_eight + offset, col_all
            )
            scale[layer, spare : spare + 8, :] = blank
        for plane in range(3 * LZ):
            e_ext[plane, target : target + 8, :] = rowh[plane, place : place + 8, :]
            h_ext[plane, target : target + 8, :] = rowh[3 * LZ + plane, place : place + 8, :]
            e_ext[plane, spare : spare + 8, :] = blank
            h_ext[plane, spare : spare + 8, :] = blank
    for plane in range(3 * LZ):
        e_ext[plane, high - 16 : high, :] = jnp.zeros((16, width), jnp.float32)
        h_ext[plane, 0:16, :] = jnp.zeros((16, width), jnp.float32)
    lane_c = lax.broadcasted_iota(jnp.int32, (CHUNK, width), 1)
    col_c = col0 + jnp.where(lane_c < cols + PAD // 2, lane_c, lane_c - width)
    weight = jnp.where(col_c >= 0, courant, 0.0)
    top = lax.axis_index("gx") == 0
    copies[0].wait()
    copies[1].wait()

    def magnetic_pass(index, carry):
        r = pl.multiple_of(index * CHUNK, CHUNK)
        now = pl.ds(r, CHUNK)
        more = pl.ds(r, CHUNK + 8)
        factor = weight * jnp.where(top & (index * CHUNK < BASE), 0.0, 1.0)
        zero = jnp.zeros((CHUNK, width), jnp.float32)
        ex = [e_ext[layer, now, :] for layer in range(LZ)] + [zero]
        ey = [e_ext[LZ + layer, now, :] for layer in range(LZ)] + [zero]
        for layer in range(LZ):
            ez = e_ext[2 * LZ + layer, now, :]
            ez_row = pltpu.roll(e_ext[2 * LZ + layer, more, :], CHUNK + 7, 0)[:CHUNK]
            ey_row = pltpu.roll(e_ext[LZ + layer, more, :], CHUNK + 7, 0)[:CHUNK]
            ez_col = pltpu.roll(ez, width - 1, 1)
            ex_col = pltpu.roll(ex[layer], width - 1, 1)
            curl_x = ez_col - ez - (ey[layer + 1] - ey[layer])
            curl_y = ex[layer + 1] - ex[layer] - (ez_row - ez)
            curl_z = ey_row - ey[layer] - (ex_col - ex[layer])
            for part, curl in enumerate((curl_x, curl_y, curl_z)):
                plane = part * LZ + layer
                h_ext[plane, now, :] = h_ext[plane, now, :] - factor * curl
        return carry

    def electric_pass(moment, last, index, carry):
        r = pl.multiple_of(index * CHUNK, CHUNK)
        now = pl.ds(r, CHUNK)
        more = pl.ds(pl.multiple_of(r - 8, 8), CHUNK + 8)
        drive = math.sin(source_rate * moment)
        zero = jnp.zeros((CHUNK, width), jnp.float32)
        hx = [zero] + [h_ext[layer, now, :] for layer in range(LZ)]
        hy = [zero] + [h_ext[LZ + layer, now, :] for layer in range(LZ)]
        for layer in range(LZ):
            hz = h_ext[2 * LZ + layer, now, :]
            hz_row = pltpu.roll(h_ext[2 * LZ + layer, more, :], 1, 0)[8:]
            hy_row = pltpu.roll(h_ext[LZ + layer, more, :], 1, 0)[8:]
            hx_now, hy_now = hx[layer + 1], hy[layer + 1]
            hz_col = pltpu.roll(hz, 1, 1)
            hx_col = pltpu.roll(hx_now, 1, 1)
            curl_x = hz - hz_col - (hy_now - hy[layer])
            curl_y = hx_now - hx[layer] - (hz - hz_row)
            curl_z = hy_now - hy_row - (hx_now - hx_col)
            factor = scale[layer, now, :]
            new_x = e_ext[layer, now, :] + factor * curl_x
            new_y = e_ext[LZ + layer, now, :] + factor * curl_y
            new_z = e_ext[2 * LZ + layer, now, :] + factor * curl_z + drive * src[layer, now, :]
            e_ext[layer, now, :] = new_x
            e_ext[LZ + layer, now, :] = new_y
            e_ext[2 * LZ + layer, now, :] = new_z
            if layer == FACE:
                faces = (-hy_now, hx_now, new_y, -new_x)
                for item, face in enumerate(faces):
                    if last:
                        old = first[item, now, :]
                        here = pl.ds(r - BASE, CHUNK)
                        span = cols // gx
                        place = (item % EACH) * span
                        for which, value in enumerate((old + face, face - old)):
                            lo = which * EACH * span + place
                            for j in range(gx):
                                piece = value[:, j * span : (j + 1) * span].astype(jnp.bfloat16)
                                sd_outs[item // EACH][j, here, lo : lo + span] = piece
                    else:
                        first[item, now, :] = face
        return carry

    chunks = high // CHUNK
    main0 = BASE // CHUNK
    main1 = main0 + rows // CHUNK
    lax.fori_loop(1, chunks - 1, magnetic_pass, 0)
    lax.fori_loop(1, chunks - 1, functools.partial(electric_pass, 1.0, False), 0)
    lax.fori_loop(1, main1, magnetic_pass, 0)
    out_h = pltpu.make_async_copy(h_ext.at[:, main_r, pl.ds(0, cols)], h_out, sems.at[3])
    out_h.start()
    lax.fori_loop(main0, main1, functools.partial(electric_pass, 2.0, True), 0)
    out_e = pltpu.make_async_copy(e_ext.at[:, main_r, pl.ds(0, cols)], e_out, sems.at[4])
    out_e.start()
    out_h.wait()
    out_e.wait()


def yee(e_field, h_field, material, eps_table, src_pos, src_amp):
    rows, cols = material.shape[1:]
    gx = lax.axis_size("gx")
    grid_rows = rows * gx
    grid_cols = cols * lax.axis_size("gy")
    planes = 3 * LZ
    e = e_field.reshape(planes, rows, cols)
    h = h_field.reshape(planes, rows, cols)

    def edge(low, high, dim):
        cut = lambda a: lax.slice_in_dim(a, low, high, axis=dim)
        return jnp.concatenate([cut(e), cut(h), cut(material).astype(jnp.float32)], 0)

    send_prev = jnp.swapaxes(edge(0, 2, 2), 1, 2)
    send_next = jnp.swapaxes(edge(cols - 2, cols, 2), 1, 2)
    right = shifted(send_prev, "gy", -1)
    left = shifted(send_next, "gy", 1)
    right = jnp.swapaxes(right, 1, 2)
    left = jnp.swapaxes(left, 1, 2)
    total = 2 * planes + LZ
    col_halo = jnp.concatenate(
        [right, jnp.zeros((total, rows, PAD - 4), jnp.float32), left], 2
    )
    send_up = jnp.concatenate([edge(0, 2, 1), col_halo[:, 0:2]], 2)
    send_down = jnp.concatenate([edge(rows - 2, rows, 1), col_halo[:, rows - 2 :]], 2)
    below = shifted(send_up, "gx", -1)
    above = shifted(send_down, "gx", 1)
    row_halo = jnp.concatenate(
        [below, jnp.zeros((total, 12, cols + PAD), jnp.float32), above], 1
    )
    high = rows + 2 * BASE
    width = cols + PAD
    f32 = jnp.float32
    out = pl.pallas_call(
        functools.partial(yee_kernel, grid_rows, grid_cols, gx),
        out_shape=(
            jax.ShapeDtypeStruct((planes, rows, cols), f32),
            jax.ShapeDtypeStruct((planes, rows, cols), f32),
        )
        + (jax.ShapeDtypeStruct((gx, rows, 2 * EACH * (cols // gx)), jnp.bfloat16),) * SETS,
        in_specs=[ANY, ANY, ANY, VM, VM, SM, VM, VM],
        out_specs=(ANY, ANY) + (VM,) * SETS,
        scratch_shapes=[
            pltpu.VMEM((planes, high, width), f32),
            pltpu.VMEM((planes, high, width), f32),
            pltpu.VMEM((LZ, rows, cols), jnp.int32),
            pltpu.VMEM((LZ, high, width), f32),
            pltpu.VMEM((LZ, high, width), f32),
            pltpu.VMEM((4, high, width), f32),
            pltpu.SemaphoreType.DMA((5,)),
        ],
        compiler_params=pltpu.CompilerParams(vmem_limit_bytes=BIG),
        name="yee",
    )(
        e, h, material, col_halo, row_halo,
        eps_table, jnp.swapaxes(src_pos, 0, 1), src_amp[None, :],
    )
    return out


def table_kernel(a_re, a_im, b_re, b_im, out):
    lo_re, lo_im = b_re[...], b_im[...]
    for block in range(a_re.shape[1]):
        hi_re = a_re[:, block : block + 1]
        hi_im = a_im[:, block : block + 1]
        at = slice(block * 128, block * 128 + 128)
        out[0, 0, :, at] = (hi_re * lo_re - hi_im * lo_im).astype(jnp.bfloat16)
        out[0, 1, :, at] = (hi_re * lo_im + hi_im * lo_re).astype(jnp.bfloat16)


def unit(phase, period):
    angle = jnp.remainder(phase, period).astype(jnp.float32) * (2.0 * math.pi / period)
    return jnp.cos(angle), -jnp.sin(angle)


def table(row_index, first, length, period, blocks):
    count = row_index.shape[0]
    high = first + 128 * jnp.arange(length // 128, dtype=jnp.int32)
    low = jnp.arange(128, dtype=jnp.int32)
    a_re, a_im = unit(row_index[:, None] * high[None, :], period)
    b_re, b_im = unit(row_index[:, None] * low[None, :], period)
    size = count // blocks
    one = pl.BlockSpec((size, length // 128), lambda i: (i, 0))
    two = pl.BlockSpec((size, 128), lambda i: (i, 0))
    return pl.pallas_call(
        table_kernel,
        grid=(blocks,),
        out_shape=jax.ShapeDtypeStruct((blocks, 2, size, length), jnp.bfloat16),
        in_specs=[one, one, two, two],
        out_specs=pl.BlockSpec((1, 2, size, length), lambda i: (i, 0, 0, 0)),
        cost_estimate=pl.CostEstimate(
            flops=8 * count * length, bytes_accessed=4 * count * length, transcendentals=0
        ),
        name="chirp",
    )(a_re, a_im, b_re, b_im)


def rows_kernel(mix, tab, v, out):
    group, _, nu, depth = tab.shape
    half = v.shape[2] // 2
    left = tab[...].reshape(group * 2 * nu, depth)
    right = v[...].reshape(depth, 2 * half)
    both = jnp.dot(left, right, preferred_element_type=jnp.float32)
    both = both.reshape(group, 2, nu, 2 * half)
    for b in range(group):
        s_re, s_im = both[b, 0, :, :half], both[b, 1, :, :half]
        d_re, d_im = both[b, 0, :, half:], both[b, 1, :, half:]
        for f in range(NF):
            p_re, p_im, q_re, q_im = (mix[f, i] for i in range(4))
            re = p_re * s_re - p_im * s_im + (q_re * d_re - q_im * d_im)
            im = p_re * s_im + p_im * s_re + (q_re * d_im + q_im * d_re)
            out[b, f, 0] = re.astype(jnp.bfloat16)
            out[b, f, 1] = im.astype(jnp.bfloat16)


def cols_kernel(g, tab, out, left):
    gx, _, _, nu, wide = g.shape
    span = wide // EACH

    @pl.when(pl.program_id(0) == 0)
    def _():
        for f in range(NF):
            for c in range(2):
                got = [g[j, f, c].astype(jnp.float32) for j in range(gx)]
                for k in range(EACH):
                    at = (f * EACH + k) * nu
                    row = [piece[:, k * span : (k + 1) * span] for piece in got]
                    left[c, at : at + nu, :] = jnp.concatenate(row, 1).astype(jnp.bfloat16)

    y_re = tab[0, 0]
    y_im = tab[0, 1]
    dot = functools.partial(jnp.dot, preferred_element_type=jnp.float32)
    re = dot(left[0], y_re) - dot(left[1], y_im)
    im = dot(left[0], y_im) + dot(left[1], y_re)
    for i in range(NF * EACH):
        out[0, i, 0] = re[i * nu : (i + 1) * nu].astype(out.dtype)
        out[0, i, 1] = im[i * nu : (i + 1) * nu].astype(out.dtype)


def on_device(e_field, h_field, material, eps_table, src_pos, src_amp, freqs):
    rows, cols = material.shape[1:]
    gx, gy = lax.axis_size("gx"), lax.axis_size("gy")
    grid_rows, grid_cols = rows * gx, cols * gy
    wide = EACH * (cols // gx)
    nu = NA // gx
    vb = NA // gy
    col_start = lax.axis_index("gy") * cols
    bf16 = jnp.bfloat16
    angle_index = jnp.arange(NA, dtype=jnp.int32)
    x_tab = table(angle_index - NA // 2, 0, grid_rows, zoom_factor * grid_rows, gx)
    y_cells = col_start + jnp.arange(cols, dtype=jnp.int32)
    y_tab = table(y_cells, NA // 4, NA, zoom_factor * grid_cols, 1)
    e_new, h_new, *sd = yee(e_field, h_field, material, eps_table, src_pos, src_amp)
    turn_re, turn_im = jnp.cos(1.5 * freqs), jnp.sin(1.5 * freqs)
    half_re, half_im = jnp.cos(0.5 * freqs), jnp.sin(0.5 * freqs)
    mix = jnp.stack(
        [turn_re * half_re, turn_im * half_re, -turn_im * half_im, turn_re * half_im], 1
    )
    group = 2
    inv_norm = 1.0 / math.sqrt(grid_rows * grid_cols)
    fars = []
    for sent in sd:
        got = lax.all_to_all(sent, "gx", split_axis=0, concat_axis=0, tiled=True)
        g = pl.pallas_call(
            rows_kernel,
            grid=(gx // group,),
            out_shape=jax.ShapeDtypeStruct((gx, NF, 2, nu, wide), bf16),
            in_specs=[
                SM,
                pl.BlockSpec((group, 2, nu, grid_rows), lambda i: (i, 0, 0, 0)),
                pl.BlockSpec((gx, rows, 2 * wide), lambda i: (0, 0, 0)),
            ],
            out_specs=pl.BlockSpec((group, NF, 2, nu, wide), lambda i: (i, 0, 0, 0, 0)),
            compiler_params=pltpu.CompilerParams(vmem_limit_bytes=BIG),
            name="rows",
        )(mix, x_tab, got)
        moved = lax.all_to_all(g, "gx", split_axis=0, concat_axis=0, tiled=True)
        share = pl.pallas_call(
            cols_kernel,
            grid=(gy,),
            out_shape=jax.ShapeDtypeStruct((gy, NF * EACH, 2, nu, vb), bf16),
            in_specs=[
                pl.BlockSpec((gx, NF, 2, nu, wide), lambda j: (0, 0, 0, 0, 0)),
                pl.BlockSpec((1, 2, cols, vb), lambda j: (0, 0, 0, j)),
            ],
            out_specs=pl.BlockSpec((1, NF * EACH, 2, nu, vb), lambda j: (j, 0, 0, 0, 0)),
            scratch_shapes=[pltpu.VMEM((2, NF * EACH * nu, cols), bf16)],
            compiler_params=pltpu.CompilerParams(vmem_limit_bytes=BIG),
            cost_estimate=pl.CostEstimate(
                flops=16 * NF * EACH * nu * cols * NA, bytes_accessed=16 * nu * NA, transcendentals=0
            ),
            name="cols",
        )(moved, y_tab)
        summed = lax.psum_scatter(share, "gy", scatter_dimension=0, tiled=True)
        scaled = summed[0].astype(jnp.float32) * inv_norm
        fars.append(jnp.transpose(scaled, (2, 0, 1, 3)).reshape(nu, NF, EACH, 2, vb))
    far = jnp.concatenate(fars, 2).reshape(nu, NF * 4, 2, vb)
    shape = e_field.shape
    return (e_new.reshape(shape), h_new.reshape(shape), far)


def solution(mesh):
    placed = (
        P(None, None, "gx", "gy"),
        P(None, None, "gx", "gy"),
        P(None, "gx", "gy"),
        P(),
        P(),
        P(),
        P(),
    )
    return jax.shard_map(
        on_device,
        mesh=mesh,
        in_specs=placed,
        out_specs=(P(None, None, "gx", "gy"), P(None, None, "gx", "gy"), P("gx", None, None, "gy")),
        check_vma=False,
    )
```

```python
import functools
import math

import jax
import jax.numpy as jnp
from jax import lax
from jax.experimental import pallas as pl
from jax.experimental.pallas import tpu as pltpu
from jax.sharding import PartitionSpec as P

LZ = 3
FACE = 1
STEPS = 2
NF = 2
NA = 1024
NMAT = 8

courant = 0.5
source_rate = 0.7
zoom_factor = 4

BASE = 32
CHUNK = 16
SETS = 2
EACH = 4 // SETS
PAD = 128
ANY = pl.BlockSpec(memory_space=pl.ANY)
VM = pl.BlockSpec(memory_space=pltpu.VMEM)
SM = pl.BlockSpec(memory_space=pltpu.SMEM)
BIG = 60 * 1024 * 1024


def shifted(block, axis, distance):
    size = lax.axis_size(axis)
    route = [(i - distance, i) for i in range(size) if 0 <= i - distance < size]
    return lax.ppermute(block, axis, route)


def yee_kernel(
    grid_rows, grid_cols, gx,
    e_hbm, h_hbm, m_hbm, colh, rowh, eps, pos, amp,
    e_out, h_out, sd_out,
    e_ext, h_ext, m_main, scale, src, first, sems,
):
    rows, cols = m_main.shape[1:]
    width = cols + PAD
    high = e_ext.shape[1]
    row0 = lax.axis_index("gx") * rows
    col0 = lax.axis_index("gy") * cols
    main_r = pl.ds(BASE, rows)
    copies = [
        pltpu.make_async_copy(e_hbm, e_ext.at[:, main_r, pl.ds(0, cols)], sems.at[0]),
        pltpu.make_async_copy(h_hbm, h_ext.at[:, main_r, pl.ds(0, cols)], sems.at[1]),
        pltpu.make_async_copy(m_hbm, m_main, sems.at[2]),
    ]
    for copy in copies:
        copy.start()
    count = amp.shape[1]
    step = min(count, 1024)
    used = high - 2 * CHUNK
    row_at = row0 + lax.broadcasted_iota(jnp.int32, (used, step), 0) + (CHUNK - BASE)
    lane = lax.broadcasted_iota(jnp.int32, (width, step), 0)
    col_at = col0 + jnp.where(lane < cols + PAD // 2, lane, lane - width)
    for start in range(0, count, step):
        at = pl.ds(start, step)
        amp_now = amp[:, at]
        hi = amp_now.astype(jnp.bfloat16).astype(jnp.float32)
        mid = (amp_now - hi).astype(jnp.bfloat16).astype(jnp.float32)
        low = amp_now - hi - mid
        hit_col = jnp.where(col_at == pos[2:3, at], 1.0, 0.0).astype(jnp.bfloat16)
        hit_row = row_at == pos[1:2, at]
        for layer in range(LZ):
            hit = hit_row & (pos[0:1, at] == layer)
            total = None
            for piece in (hi, mid, low):
                left = jnp.where(hit, piece, 0.0).astype(jnp.bfloat16)
                term = lax.dot_general(
                    left, hit_col, (((1,), (1,)), ((), ())), preferred_element_type=jnp.float32
                )
                total = term if total is None else total + term
            if start == 0:
                src[layer, CHUNK : CHUNK + used, :] = total
            else:
                src[layer, CHUNK : CHUNK + used, :] += total
    copies[2].wait()

    def scale_of(index, row, col):
        value = jnp.full(index.shape, eps[0], jnp.float32)
        for material in range(1, NMAT):
            value = jnp.where(index == material, eps[material], value)
        inside = (row >= 0) & (row < grid_rows) & (col >= 0) & (col < grid_cols)
        return jnp.where(inside, courant / value, 0.0)

    col_main = col0 + lax.broadcasted_iota(jnp.int32, (CHUNK, cols), 1)
    lane_pad = lax.broadcasted_iota(jnp.int32, (CHUNK, PAD), 1)
    col_pad = col0 + jnp.where(lane_pad < PAD // 2, cols + lane_pad, lane_pad - PAD)
    row_chunk = row0 + lax.broadcasted_iota(jnp.int32, (CHUNK, cols), 0)

    def fill(step_index, carry):
        r = pl.multiple_of(step_index * CHUNK, CHUNK)
        near = pl.ds(r, CHUNK)
        far = pl.ds(BASE + r, CHUNK)
        for layer in range(LZ):
            scale[layer, far, :cols] = scale_of(m_main[layer, near, :], row_chunk + r, col_main)
            scale[layer, far, cols:] = scale_of(
                colh[6 * LZ + layer, near, :], row_chunk[:, :PAD] + r, col_pad
            )
        for plane in range(3 * LZ):
            e_ext[plane, far, cols:] = colh[plane, near, :]
            h_ext[plane, far, cols:] = colh[3 * LZ + plane, near, :]
        return carry

    lax.fori_loop(0, rows // CHUNK, fill, 0)
    lane_all = lax.broadcasted_iota(jnp.int32, (8, width), 1)
    col_all = col0 + jnp.where(lane_all < cols + PAD // 2, lane_all, lane_all - width)
    row_eight = row0 + lax.broadcasted_iota(jnp.int32, (8, width), 0)
    blank = jnp.zeros((8, width), jnp.float32)
    for place, target, offset, spare in (
        (0, BASE + rows, rows, BASE + rows + 8),
        (8, BASE - 8, -8, BASE - 16),
    ):
        for layer in range(LZ):
            scale[layer, target : target + 8, :] = scale_of(
                rowh[6 * LZ + layer, place : place + 8, :], row_eight + offset, col_all
            )
            scale[layer, spare : spare + 8, :] = blank
        for plane in range(3 * LZ):
            e_ext[plane, target : target + 8, :] = rowh[plane, place : place + 8, :]
            h_ext[plane, target : target + 8, :] = rowh[3 * LZ + plane, place : place + 8, :]
            e_ext[plane, spare : spare + 8, :] = blank
            h_ext[plane, spare : spare + 8, :] = blank
    for plane in range(3 * LZ):
        e_ext[plane, high - 16 : high, :] = jnp.zeros((16, width), jnp.float32)
        h_ext[plane, 0:16, :] = jnp.zeros((16, width), jnp.float32)
    lane_c = lax.broadcasted_iota(jnp.int32, (CHUNK, width), 1)
    col_c = col0 + jnp.where(lane_c < cols + PAD // 2, lane_c, lane_c - width)
    weight = jnp.where(col_c >= 0, courant, 0.0)
    top = lax.axis_index("gx") == 0
    copies[0].wait()
    copies[1].wait()

    def magnetic_pass(index, carry):
        r = pl.multiple_of(index * CHUNK, CHUNK)
        now = pl.ds(r, CHUNK)
        more = pl.ds(r, CHUNK + 8)
        factor = weight * jnp.where(top & (index * CHUNK < BASE), 0.0, 1.0)
        zero = jnp.zeros((CHUNK, width), jnp.float32)
        ex = [e_ext[layer, now, :] for layer in range(LZ)] + [zero]
        ey = [e_ext[LZ + layer, now, :] for layer in range(LZ)] + [zero]
        for layer in range(LZ):
            ez = e_ext[2 * LZ + layer, now, :]
            ez_row = pltpu.roll(e_ext[2 * LZ + layer, more, :], CHUNK + 7, 0)[:CHUNK]
            ey_row = pltpu.roll(e_ext[LZ + layer, more, :], CHUNK + 7, 0)[:CHUNK]
            ez_col = pltpu.roll(ez, width - 1, 1)
            ex_col = pltpu.roll(ex[layer], width - 1, 1)
            curl_x = ez_col - ez - (ey[layer + 1] - ey[layer])
            curl_y = ex[layer + 1] - ex[layer] - (ez_row - ez)
            curl_z = ey_row - ey[layer] - (ex_col - ex[layer])
            for part, curl in enumerate((curl_x, curl_y, curl_z)):
                plane = part * LZ + layer
                h_ext[plane, now, :] = h_ext[plane, now, :] - factor * curl
        return carry

    def electric_pass(moment, last, index, carry):
        r = pl.multiple_of(index * CHUNK, CHUNK)
        now = pl.ds(r, CHUNK)
        more = pl.ds(pl.multiple_of(r - 8, 8), CHUNK + 8)
        drive = math.sin(source_rate * moment)
        zero = jnp.zeros((CHUNK, width), jnp.float32)
        hx = [zero] + [h_ext[layer, now, :] for layer in range(LZ)]
        hy = [zero] + [h_ext[LZ + layer, now, :] for layer in range(LZ)]
        for layer in range(LZ):
            hz = h_ext[2 * LZ + layer, now, :]
            hz_row = pltpu.roll(h_ext[2 * LZ + layer, more, :], 1, 0)[8:]
            hy_row = pltpu.roll(h_ext[LZ + layer, more, :], 1, 0)[8:]
            hx_now, hy_now = hx[layer + 1], hy[layer + 1]
            hz_col = pltpu.roll(hz, 1, 1)
            hx_col = pltpu.roll(hx_now, 1, 1)
            curl_x = hz - hz_col - (hy_now - hy[layer])
            curl_y = hx_now - hx[layer] - (hz - hz_row)
            curl_z = hy_now - hy_row - (hx_now - hx_col)
            factor = scale[layer, now, :]
            new_x = e_ext[layer, now, :] + factor * curl_x
            new_y = e_ext[LZ + layer, now, :] + factor * curl_y
            new_z = e_ext[2 * LZ + layer, now, :] + factor * curl_z + drive * src[layer, now, :]
            e_ext[layer, now, :] = new_x
            e_ext[LZ + layer, now, :] = new_y
            e_ext[2 * LZ + layer, now, :] = new_z
            if layer == FACE:
                faces = (-hy_now, hx_now, new_y, -new_x)
                for item, face in enumerate(faces):
                    if last:
                        old = first[item, now, :]
                        here = pl.ds(
                            pl.multiple_of(r - BASE + item // EACH * rows, CHUNK), CHUNK
                        )
                        span = cols // gx
                        place = (item % EACH) * span
                        for which, value in enumerate((old + face, face - old)):
                            lo = which * EACH * span + place
                            for j in range(gx):
                                piece = value[:, j * span : (j + 1) * span].astype(jnp.bfloat16)
                                sd_out[j, here, lo : lo + span] = piece
                    else:
                        first[item, now, :] = face
        return carry

    chunks = high // CHUNK
    main0 = BASE // CHUNK
    main1 = main0 + rows // CHUNK
    lax.fori_loop(1, chunks - 1, magnetic_pass, 0)
    lax.fori_loop(1, chunks - 1, functools.partial(electric_pass, 1.0, False), 0)
    lax.fori_loop(1, main1, magnetic_pass, 0)
    out_h = pltpu.make_async_copy(h_ext.at[:, main_r, pl.ds(0, cols)], h_out, sems.at[3])
    out_h.start()
    lax.fori_loop(main0, main1, functools.partial(electric_pass, 2.0, True), 0)
    out_e = pltpu.make_async_copy(e_ext.at[:, main_r, pl.ds(0, cols)], e_out, sems.at[4])
    out_e.start()
    out_h.wait()
    out_e.wait()


def yee(e_field, h_field, material, eps_table, src_pos, src_amp):
    rows, cols = material.shape[1:]
    gx = lax.axis_size("gx")
    grid_rows = rows * gx
    grid_cols = cols * lax.axis_size("gy")
    planes = 3 * LZ
    e = e_field.reshape(planes, rows, cols)
    h = h_field.reshape(planes, rows, cols)

    def edge(low, high, dim):
        cut = lambda a: lax.slice_in_dim(a, low, high, axis=dim)
        return jnp.concatenate([cut(e), cut(h), cut(material).astype(jnp.float32)], 0)

    send_prev = jnp.swapaxes(edge(0, 2, 2), 1, 2)
    send_next = jnp.swapaxes(edge(cols - 2, cols, 2), 1, 2)
    right = shifted(send_prev, "gy", -1)
    left = shifted(send_next, "gy", 1)
    right = jnp.swapaxes(right, 1, 2)
    left = jnp.swapaxes(left, 1, 2)
    total = 2 * planes + LZ
    col_halo = jnp.concatenate(
        [right, jnp.zeros((total, rows, PAD - 4), jnp.float32), left], 2
    )
    send_up = jnp.concatenate([edge(0, 2, 1), col_halo[:, 0:2]], 2)
    send_down = jnp.concatenate([edge(rows - 2, rows, 1), col_halo[:, rows - 2 :]], 2)
    below = shifted(send_up, "gx", -1)
    above = shifted(send_down, "gx", 1)
    row_halo = jnp.concatenate(
        [below, jnp.zeros((total, 12, cols + PAD), jnp.float32), above], 1
    )
    high = rows + 2 * BASE
    width = cols + PAD
    f32 = jnp.float32
    out = pl.pallas_call(
        functools.partial(yee_kernel, grid_rows, grid_cols, gx),
        out_shape=(
            jax.ShapeDtypeStruct((planes, rows, cols), f32),
            jax.ShapeDtypeStruct((planes, rows, cols), f32),
        )
        + (jax.ShapeDtypeStruct((gx, SETS * rows, 2 * EACH * (cols // gx)), jnp.bfloat16),),
        in_specs=[ANY, ANY, ANY, VM, VM, SM, VM, VM],
        out_specs=(ANY, ANY, VM),
        scratch_shapes=[
            pltpu.VMEM((planes, high, width), f32),
            pltpu.VMEM((planes, high, width), f32),
            pltpu.VMEM((LZ, rows, cols), jnp.int32),
            pltpu.VMEM((LZ, high, width), f32),
            pltpu.VMEM((LZ, high, width), f32),
            pltpu.VMEM((4, high, width), f32),
            pltpu.SemaphoreType.DMA((5,)),
        ],
        compiler_params=pltpu.CompilerParams(vmem_limit_bytes=BIG),
        name="yee",
    )(
        e, h, material, col_halo, row_halo,
        eps_table, jnp.swapaxes(src_pos, 0, 1), src_amp[None, :],
    )
    return out


def table_kernel(a_re, a_im, b_re, b_im, out):
    lo_re, lo_im = b_re[...], b_im[...]
    for block in range(a_re.shape[1]):
        hi_re = a_re[:, block : block + 1]
        hi_im = a_im[:, block : block + 1]
        at = slice(block * 128, block * 128 + 128)
        out[0, 0, :, at] = (hi_re * lo_re - hi_im * lo_im).astype(jnp.bfloat16)
        out[0, 1, :, at] = (hi_re * lo_im + hi_im * lo_re).astype(jnp.bfloat16)


def unit(phase, period):
    angle = jnp.remainder(phase, period).astype(jnp.float32) * (2.0 * math.pi / period)
    return jnp.cos(angle), -jnp.sin(angle)


def table(row_index, first, length, period, blocks):
    count = row_index.shape[0]
    high = first + 128 * jnp.arange(length // 128, dtype=jnp.int32)
    low = jnp.arange(128, dtype=jnp.int32)
    a_re, a_im = unit(row_index[:, None] * high[None, :], period)
    b_re, b_im = unit(row_index[:, None] * low[None, :], period)
    size = count // blocks
    one = pl.BlockSpec((size, length // 128), lambda i: (i, 0))
    two = pl.BlockSpec((size, 128), lambda i: (i, 0))
    return pl.pallas_call(
        table_kernel,
        grid=(blocks,),
        out_shape=jax.ShapeDtypeStruct((blocks, 2, size, length), jnp.bfloat16),
        in_specs=[one, one, two, two],
        out_specs=pl.BlockSpec((1, 2, size, length), lambda i: (i, 0, 0, 0)),
        cost_estimate=pl.CostEstimate(
            flops=8 * count * length, bytes_accessed=4 * count * length, transcendentals=0
        ),
        name="chirp",
    )(a_re, a_im, b_re, b_im)


def rows_kernel(mix, tab, v, *outs):
    group, _, nu, depth = tab.shape
    half = v.shape[2] // 2
    left = tab[...].reshape(group * 2 * nu, depth)
    right = v[...].reshape(depth, 2 * half)
    both = jnp.dot(left, right, preferred_element_type=jnp.float32)
    both = both.reshape(group, 2, nu, 2 * half)
    for b in range(group):
        s_re, s_im = both[b, 0, :, :half], both[b, 1, :, :half]
        d_re, d_im = both[b, 0, :, half:], both[b, 1, :, half:]
        for f in range(NF):
            p_re, p_im, q_re, q_im = (mix[f, i] for i in range(4))
            re = p_re * s_re - p_im * s_im + (q_re * d_re - q_im * d_im)
            im = p_re * s_im + p_im * s_re + (q_re * d_im + q_im * d_re)
            outs[f][b, 0] = re.astype(jnp.bfloat16)
            outs[f][b, 1] = im.astype(jnp.bfloat16)


def cols_kernel(g, tab, out, left):
    gx, _, nu, wide = g.shape
    span = wide // EACH

    @pl.when(pl.program_id(0) == 0)
    def _():
        for c in range(2):
            got = [g[j, c].astype(jnp.float32) for j in range(gx)]
            for k in range(EACH):
                row = [piece[:, k * span : (k + 1) * span] for piece in got]
                left[c, k * nu : (k + 1) * nu, :] = jnp.concatenate(row, 1).astype(jnp.bfloat16)

    y_re = tab[0, 0]
    y_im = tab[0, 1]
    dot = functools.partial(jnp.dot, preferred_element_type=jnp.float32)
    re = dot(left[0], y_re) - dot(left[1], y_im)
    im = dot(left[0], y_im) + dot(left[1], y_re)
    for i in range(EACH):
        out[0, i, 0] = re[i * nu : (i + 1) * nu].astype(out.dtype)
        out[0, i, 1] = im[i * nu : (i + 1) * nu].astype(out.dtype)


def on_device(e_field, h_field, material, eps_table, src_pos, src_amp, freqs):
    rows, cols = material.shape[1:]
    gx, gy = lax.axis_size("gx"), lax.axis_size("gy")
    grid_rows, grid_cols = rows * gx, cols * gy
    wide = EACH * (cols // gx)
    nu = NA // gx
    vb = NA // gy
    col_start = lax.axis_index("gy") * cols
    bf16 = jnp.bfloat16
    angle_index = jnp.arange(NA, dtype=jnp.int32)
    x_tab = table(angle_index - NA // 2, 0, grid_rows, zoom_factor * grid_rows, gx)
    y_cells = col_start + jnp.arange(cols, dtype=jnp.int32)
    y_tab = table(y_cells, NA // 4, NA, zoom_factor * grid_cols, 1)
    e_new, h_new, sd = yee(e_field, h_field, material, eps_table, src_pos, src_amp)
    turn_re, turn_im = jnp.cos(1.5 * freqs), jnp.sin(1.5 * freqs)
    half_re, half_im = jnp.cos(0.5 * freqs), jnp.sin(0.5 * freqs)
    mix = jnp.stack(
        [turn_re * half_re, turn_im * half_re, -turn_im * half_im, turn_re * half_im], 1
    )
    group = 2
    inv_norm = 1.0 / math.sqrt(grid_rows * grid_cols)
    got = lax.all_to_all(sd, "gx", split_axis=0, concat_axis=0, tiled=True)
    fars = []
    for group_at in range(SETS):
        halves = pl.pallas_call(
            rows_kernel,
            grid=(gx // group,),
            out_shape=[jax.ShapeDtypeStruct((gx, 2, nu, wide), bf16)] * NF,
            in_specs=[
                SM,
                pl.BlockSpec((group, 2, nu, grid_rows), lambda i: (i, 0, 0, 0)),
                pl.BlockSpec((gx, rows, 2 * wide), lambda i, at=group_at: (0, at, 0)),
            ],
            out_specs=[pl.BlockSpec((group, 2, nu, wide), lambda i: (i, 0, 0, 0))] * NF,
            compiler_params=pltpu.CompilerParams(vmem_limit_bytes=BIG),
            cost_estimate=pl.CostEstimate(
                flops=8 * NA * grid_rows * wide,
                bytes_accessed=4 * NA * grid_rows,
                transcendentals=0,
            ),
            name="rows",
        )(mix, x_tab, got)
        done = []
        for g in halves:
            moved = lax.all_to_all(g, "gx", split_axis=0, concat_axis=0, tiled=True)
            share = pl.pallas_call(
                cols_kernel,
                grid=(gy,),
                out_shape=jax.ShapeDtypeStruct((gy, EACH, 2, nu, vb), bf16),
                in_specs=[
                    pl.BlockSpec((gx, 2, nu, wide), lambda j: (0, 0, 0, 0)),
                    pl.BlockSpec((1, 2, cols, vb), lambda j: (0, 0, 0, j)),
                ],
                out_specs=pl.BlockSpec((1, EACH, 2, nu, vb), lambda j: (j, 0, 0, 0, 0)),
                scratch_shapes=[pltpu.VMEM((2, EACH * nu, cols), bf16)],
                compiler_params=pltpu.CompilerParams(vmem_limit_bytes=BIG),
                cost_estimate=pl.CostEstimate(
                    flops=8 * EACH * nu * cols * NA, bytes_accessed=16 * nu * NA, transcendentals=0
                ),
                name="cols",
            )(moved, y_tab)
            summed = lax.psum_scatter(share, "gy", scatter_dimension=0, tiled=True)
            scaled = summed[0].astype(jnp.float32) * inv_norm
            done.append(jnp.transpose(scaled, (2, 0, 1, 3)))
        fars.append(done)
    far = jnp.concatenate([fars[at][f] for f in range(NF) for at in range(SETS)], 1)
    shape = e_field.shape
    return (e_new.reshape(shape), h_new.reshape(shape), far)


def solution(mesh):
    placed = (
        P(None, None, "gx", "gy"),
        P(None, None, "gx", "gy"),
        P(None, "gx", "gy"),
        P(),
        P(),
        P(),
        P(),
    )
    return jax.shard_map(
        on_device,
        mesh=mesh,
        in_specs=placed,
        out_specs=(P(None, None, "gx", "gy"), P(None, None, "gx", "gy"), P("gx", None, None, "gy")),
        check_vma=False,
    )
```

```python
import functools
import math

import jax
import jax.numpy as jnp
from jax import lax
from jax.experimental import pallas as pl
from jax.experimental.pallas import tpu as pltpu
from jax.sharding import PartitionSpec as P

LZ = 3
FACE = 1
STEPS = 2
NF = 2
NA = 1024
NMAT = 8

courant = 0.5
source_rate = 0.7
zoom_factor = 4

BASE = 32
CHUNK = 16
SETS = 2
EACH = 4 // SETS
PAD = 128
ANY = pl.BlockSpec(memory_space=pl.ANY)
VM = pl.BlockSpec(memory_space=pltpu.VMEM)
SM = pl.BlockSpec(memory_space=pltpu.SMEM)
BIG = 60 * 1024 * 1024


def shifted(block, axis, distance):
    size = lax.axis_size(axis)
    route = [(i - distance, i) for i in range(size) if 0 <= i - distance < size]
    return lax.ppermute(block, axis, route)


def yee_kernel(
    grid_rows, grid_cols, gx,
    e_hbm, h_hbm, m_hbm, colh, rowh, eps, pos, amp,
    e_out, h_out, *rest,
):
    sd_outs, (e_ext, h_ext, m_main, scale, src, first, sems) = rest[:SETS], rest[SETS:]
    rows, cols = m_main.shape[1:]
    width = cols + PAD
    high = e_ext.shape[1]
    row0 = lax.axis_index("gx") * rows
    col0 = lax.axis_index("gy") * cols
    main_r = pl.ds(BASE, rows)
    copies = [
        pltpu.make_async_copy(e_hbm, e_ext.at[:, main_r, pl.ds(0, cols)], sems.at[0]),
        pltpu.make_async_copy(h_hbm, h_ext.at[:, main_r, pl.ds(0, cols)], sems.at[1]),
        pltpu.make_async_copy(m_hbm, m_main, sems.at[2]),
    ]
    for copy in copies:
        copy.start()
    count = amp.shape[1]
    step = min(count, 1024)
    used = high - 2 * CHUNK
    row_at = row0 + lax.broadcasted_iota(jnp.int32, (used, step), 0) + (CHUNK - BASE)
    lane = lax.broadcasted_iota(jnp.int32, (width, step), 0)
    col_at = col0 + jnp.where(lane < cols + PAD // 2, lane, lane - width)
    for start in range(0, count, step):
        at = pl.ds(start, step)
        amp_now = amp[:, at]
        hi = amp_now.astype(jnp.bfloat16).astype(jnp.float32)
        mid = (amp_now - hi).astype(jnp.bfloat16).astype(jnp.float32)
        low = amp_now - hi - mid
        hit_col = jnp.where(col_at == pos[2:3, at], 1.0, 0.0).astype(jnp.bfloat16)
        hit_row = row_at == pos[1:2, at]
        for layer in range(LZ):
            hit = hit_row & (pos[0:1, at] == layer)
            total = None
            for piece in (hi, mid, low):
                left = jnp.where(hit, piece, 0.0).astype(jnp.bfloat16)
                term = lax.dot_general(
                    left, hit_col, (((1,), (1,)), ((), ())), preferred_element_type=jnp.float32
                )
                total = term if total is None else total + term
            if start == 0:
                src[layer, CHUNK : CHUNK + used, :] = total
            else:
                src[layer, CHUNK : CHUNK + used, :] += total
    copies[2].wait()

    def scale_of(index, row, col):
        value = jnp.full(index.shape, eps[0], jnp.float32)
        for material in range(1, NMAT):
            value = jnp.where(index == material, eps[material], value)
        inside = (row >= 0) & (row < grid_rows) & (col >= 0) & (col < grid_cols)
        return jnp.where(inside, courant / value, 0.0)

    col_main = col0 + lax.broadcasted_iota(jnp.int32, (CHUNK, cols), 1)
    lane_pad = lax.broadcasted_iota(jnp.int32, (CHUNK, PAD), 1)
    col_pad = col0 + jnp.where(lane_pad < PAD // 2, cols + lane_pad, lane_pad - PAD)
    row_chunk = row0 + lax.broadcasted_iota(jnp.int32, (CHUNK, cols), 0)

    def fill(step_index, carry):
        r = pl.multiple_of(step_index * CHUNK, CHUNK)
        near = pl.ds(r, CHUNK)
        far = pl.ds(BASE + r, CHUNK)
        for layer in range(LZ):
            scale[layer, far, :cols] = scale_of(m_main[layer, near, :], row_chunk + r, col_main)
            scale[layer, far, cols:] = scale_of(
                colh[6 * LZ + layer, near, :], row_chunk[:, :PAD] + r, col_pad
            )
        for plane in range(3 * LZ):
            e_ext[plane, far, cols:] = colh[plane, near, :]
            h_ext[plane, far, cols:] = colh[3 * LZ + plane, near, :]
        return carry

    lax.fori_loop(0, rows // CHUNK, fill, 0)
    lane_all = lax.broadcasted_iota(jnp.int32, (8, width), 1)
    col_all = col0 + jnp.where(lane_all < cols + PAD // 2, lane_all, lane_all - width)
    row_eight = row0 + lax.broadcasted_iota(jnp.int32, (8, width), 0)
    blank = jnp.zeros((8, width), jnp.float32)
    for place, target, offset, spare in (
        (0, BASE + rows, rows, BASE + rows + 8),
        (8, BASE - 8, -8, BASE - 16),
    ):
        for layer in range(LZ):
            scale[layer, target : target + 8, :] = scale_of(
                rowh[6 * LZ + layer, place : place + 8, :], row_eight + offset, col_all
            )
            scale[layer, spare : spare + 8, :] = blank
        for plane in range(3 * LZ):
            e_ext[plane, target : target + 8, :] = rowh[plane, place : place + 8, :]
            h_ext[plane, target : target + 8, :] = rowh[3 * LZ + plane, place : place + 8, :]
            e_ext[plane, spare : spare + 8, :] = blank
            h_ext[plane, spare : spare + 8, :] = blank
    for plane in range(3 * LZ):
        e_ext[plane, high - 16 : high, :] = jnp.zeros((16, width), jnp.float32)
        h_ext[plane, 0:16, :] = jnp.zeros((16, width), jnp.float32)
    lane_c = lax.broadcasted_iota(jnp.int32, (CHUNK, width), 1)
    col_c = col0 + jnp.where(lane_c < cols + PAD // 2, lane_c, lane_c - width)
    weight = jnp.where(col_c >= 0, courant, 0.0)
    top = lax.axis_index("gx") == 0
    copies[0].wait()
    copies[1].wait()

    def magnetic_pass(index, carry):
        r = pl.multiple_of(index * CHUNK, CHUNK)
        now = pl.ds(r, CHUNK)
        more = pl.ds(r, CHUNK + 8)
        factor = weight * jnp.where(top & (index * CHUNK < BASE), 0.0, 1.0)
        zero = jnp.zeros((CHUNK, width), jnp.float32)
        ex = [e_ext[layer, now, :] for layer in range(LZ)] + [zero]
        ey = [e_ext[LZ + layer, now, :] for layer in range(LZ)] + [zero]
        for layer in range(LZ):
            ez = e_ext[2 * LZ + layer, now, :]
            ez_row = pltpu.roll(e_ext[2 * LZ + layer, more, :], CHUNK + 7, 0)[:CHUNK]
            ey_row = pltpu.roll(e_ext[LZ + layer, more, :], CHUNK + 7, 0)[:CHUNK]
            ez_col = pltpu.roll(ez, width - 1, 1)
            ex_col = pltpu.roll(ex[layer], width - 1, 1)
            curl_x = ez_col - ez - (ey[layer + 1] - ey[layer])
            curl_y = ex[layer + 1] - ex[layer] - (ez_row - ez)
            curl_z = ey_row - ey[layer] - (ex_col - ex[layer])
            for part, curl in enumerate((curl_x, curl_y, curl_z)):
                plane = part * LZ + layer
                h_ext[plane, now, :] = h_ext[plane, now, :] - factor * curl
        return carry

    def electric_pass(moment, last, index, carry):
        r = pl.multiple_of(index * CHUNK, CHUNK)
        now = pl.ds(r, CHUNK)
        more = pl.ds(pl.multiple_of(r - 8, 8), CHUNK + 8)
        drive = math.sin(source_rate * moment)
        zero = jnp.zeros((CHUNK, width), jnp.float32)
        hx = [zero] + [h_ext[layer, now, :] for layer in range(LZ)]
        hy = [zero] + [h_ext[LZ + layer, now, :] for layer in range(LZ)]
        for layer in range(LZ):
            hz = h_ext[2 * LZ + layer, now, :]
            hz_row = pltpu.roll(h_ext[2 * LZ + layer, more, :], 1, 0)[8:]
            hy_row = pltpu.roll(h_ext[LZ + layer, more, :], 1, 0)[8:]
            hx_now, hy_now = hx[layer + 1], hy[layer + 1]
            hz_col = pltpu.roll(hz, 1, 1)
            hx_col = pltpu.roll(hx_now, 1, 1)
            curl_x = hz - hz_col - (hy_now - hy[layer])
            curl_y = hx_now - hx[layer] - (hz - hz_row)
            curl_z = hy_now - hy_row - (hx_now - hx_col)
            factor = scale[layer, now, :]
            new_x = e_ext[layer, now, :] + factor * curl_x
            new_y = e_ext[LZ + layer, now, :] + factor * curl_y
            new_z = e_ext[2 * LZ + layer, now, :] + factor * curl_z + drive * src[layer, now, :]
            e_ext[layer, now, :] = new_x
            e_ext[LZ + layer, now, :] = new_y
            e_ext[2 * LZ + layer, now, :] = new_z
            if layer == FACE:
                faces = (-hy_now, hx_now, new_y, -new_x)
                for item, face in enumerate(faces):
                    if last:
                        old = first[item, now, :]
                        here = pl.ds(r - BASE, CHUNK)
                        span = cols // gx
                        place = (item % EACH) * span
                        for which, value in enumerate((old + face, face - old)):
                            lo = which * EACH * span + place
                            for j in range(gx):
                                piece = value[:, j * span : (j + 1) * span].astype(jnp.bfloat16)
                                sd_outs[item // EACH][j, here, lo : lo + span] = piece
                    else:
                        first[item, now, :] = face
        return carry

    chunks = high // CHUNK
    main0 = BASE // CHUNK
    main1 = main0 + rows // CHUNK
    lax.fori_loop(1, chunks - 1, magnetic_pass, 0)
    lax.fori_loop(1, chunks - 1, functools.partial(electric_pass, 1.0, False), 0)
    lax.fori_loop(1, main1, magnetic_pass, 0)
    out_h = pltpu.make_async_copy(h_ext.at[:, main_r, pl.ds(0, cols)], h_out, sems.at[3])
    out_h.start()
    lax.fori_loop(main0, main1, functools.partial(electric_pass, 2.0, True), 0)
    out_e = pltpu.make_async_copy(e_ext.at[:, main_r, pl.ds(0, cols)], e_out, sems.at[4])
    out_e.start()
    out_h.wait()
    out_e.wait()


def yee(e_field, h_field, material, eps_table, src_pos, src_amp):
    rows, cols = material.shape[1:]
    gx = lax.axis_size("gx")
    grid_rows = rows * gx
    grid_cols = cols * lax.axis_size("gy")
    planes = 3 * LZ
    e = e_field.reshape(planes, rows, cols)
    h = h_field.reshape(planes, rows, cols)

    def edge(low, high, dim):
        cut = lambda a: lax.slice_in_dim(a, low, high, axis=dim)
        return jnp.concatenate([cut(e), cut(h), cut(material).astype(jnp.float32)], 0)

    send_prev = jnp.swapaxes(edge(0, 2, 2), 1, 2)
    send_next = jnp.swapaxes(edge(cols - 2, cols, 2), 1, 2)
    right = shifted(send_prev, "gy", -1)
    left = shifted(send_next, "gy", 1)
    right = jnp.swapaxes(right, 1, 2)
    left = jnp.swapaxes(left, 1, 2)
    total = 2 * planes + LZ
    col_halo = jnp.concatenate(
        [right, jnp.zeros((total, rows, PAD - 4), jnp.float32), left], 2
    )
    send_up = jnp.concatenate([edge(0, 2, 1), col_halo[:, 0:2]], 2)
    send_down = jnp.concatenate([edge(rows - 2, rows, 1), col_halo[:, rows - 2 :]], 2)
    below = shifted(send_up, "gx", -1)
    above = shifted(send_down, "gx", 1)
    row_halo = jnp.concatenate(
        [below, jnp.zeros((total, 12, cols + PAD), jnp.float32), above], 1
    )
    high = rows + 2 * BASE
    width = cols + PAD
    f32 = jnp.float32
    out = pl.pallas_call(
        functools.partial(yee_kernel, grid_rows, grid_cols, gx),
        out_shape=(
            jax.ShapeDtypeStruct((planes, rows, cols), f32),
            jax.ShapeDtypeStruct((planes, rows, cols), f32),
        )
        + (jax.ShapeDtypeStruct((gx, rows, 2 * EACH * (cols // gx)), jnp.bfloat16),) * SETS,
        in_specs=[ANY, ANY, ANY, VM, VM, SM, VM, VM],
        out_specs=(ANY, ANY) + (VM,) * SETS,
        scratch_shapes=[
            pltpu.VMEM((planes, high, width), f32),
            pltpu.VMEM((planes, high, width), f32),
            pltpu.VMEM((LZ, rows, cols), jnp.int32),
            pltpu.VMEM((LZ, high, width), f32),
            pltpu.VMEM((LZ, high, width), f32),
            pltpu.VMEM((4, high, width), f32),
            pltpu.SemaphoreType.DMA((5,)),
        ],
        compiler_params=pltpu.CompilerParams(vmem_limit_bytes=BIG),
        name="yee",
    )(
        e, h, material, col_halo, row_halo,
        eps_table, jnp.swapaxes(src_pos, 0, 1), src_amp[None, :],
    )
    return out


def table_kernel(a_re, a_im, b_re, b_im, out):
    lo_re, lo_im = b_re[...], b_im[...]
    for block in range(a_re.shape[1]):
        hi_re = a_re[:, block : block + 1]
        hi_im = a_im[:, block : block + 1]
        at = slice(block * 128, block * 128 + 128)
        out[0, 0, :, at] = (hi_re * lo_re - hi_im * lo_im).astype(jnp.bfloat16)
        out[0, 1, :, at] = (hi_re * lo_im + hi_im * lo_re).astype(jnp.bfloat16)


def unit(phase, period):
    angle = jnp.remainder(phase, period).astype(jnp.float32) * (2.0 * math.pi / period)
    return jnp.cos(angle), -jnp.sin(angle)


def table(row_index, first, length, period, blocks):
    count = row_index.shape[0]
    high = first + 128 * jnp.arange(length // 128, dtype=jnp.int32)
    low = jnp.arange(128, dtype=jnp.int32)
    a_re, a_im = unit(row_index[:, None] * high[None, :], period)
    b_re, b_im = unit(row_index[:, None] * low[None, :], period)
    size = count // blocks
    one = pl.BlockSpec((size, length // 128), lambda i: (i, 0))
    two = pl.BlockSpec((size, 128), lambda i: (i, 0))
    return pl.pallas_call(
        table_kernel,
        grid=(blocks,),
        out_shape=jax.ShapeDtypeStruct((blocks, 2, size, length), jnp.bfloat16),
        in_specs=[one, one, two, two],
        out_specs=pl.BlockSpec((1, 2, size, length), lambda i: (i, 0, 0, 0)),
        cost_estimate=pl.CostEstimate(
            flops=8 * count * length, bytes_accessed=4 * count * length, transcendentals=0
        ),
        name="chirp",
    )(a_re, a_im, b_re, b_im)


def rows_kernel(mix, tab, v, out):
    group, _, nu, depth = tab.shape
    half = v.shape[2] // 2
    left = tab[...].reshape(group * 2 * nu, depth)
    right = v[...].reshape(depth, 2 * half)
    both = jnp.dot(left, right, preferred_element_type=jnp.float32)
    both = both.reshape(group, 2, nu, 2 * half)
    for b in range(group):
        s_re, s_im = both[b, 0, :, :half], both[b, 1, :, :half]
        d_re, d_im = both[b, 0, :, half:], both[b, 1, :, half:]
        for f in range(NF):
            p_re, p_im, q_re, q_im = (mix[f, i] for i in range(4))
            re = p_re * s_re - p_im * s_im + (q_re * d_re - q_im * d_im)
            im = p_re * s_im + p_im * s_re + (q_re * d_im + q_im * d_re)
            out[b, f, 0] = re.astype(jnp.bfloat16)
            out[b, f, 1] = im.astype(jnp.bfloat16)


def cols_kernel(g, tab, out, left):
    gx, _, _, nu, wide = g.shape
    span = wide // EACH

    @pl.when(pl.program_id(0) == 0)
    def _():
        for f in range(NF):
            for c in range(2):
                got = [g[j, f, c].astype(jnp.float32) for j in range(gx)]
                for k in range(EACH):
                    at = (f * EACH + k) * nu
                    row = [piece[:, k * span : (k + 1) * span] for piece in got]
                    left[c, at : at + nu, :] = jnp.concatenate(row, 1).astype(jnp.bfloat16)

    y_re = tab[0, 0]
    y_im = tab[0, 1]
    dot = functools.partial(jnp.dot, preferred_element_type=jnp.float32)
    re = dot(left[0], y_re) - dot(left[1], y_im)
    im = dot(left[0], y_im) + dot(left[1], y_re)
    for i in range(NF * EACH):
        out[0, i, 0] = re[i * nu : (i + 1) * nu].astype(out.dtype)
        out[0, i, 1] = im[i * nu : (i + 1) * nu].astype(out.dtype)


def on_device(e_field, h_field, material, eps_table, src_pos, src_amp, freqs):
    rows, cols = material.shape[1:]
    gx, gy = lax.axis_size("gx"), lax.axis_size("gy")
    grid_rows, grid_cols = rows * gx, cols * gy
    wide = EACH * (cols // gx)
    nu = NA // gx
    vb = NA // gy
    col_start = lax.axis_index("gy") * cols
    bf16 = jnp.bfloat16
    angle_index = jnp.arange(NA, dtype=jnp.int32)
    x_tab = table(angle_index - NA // 2, 0, grid_rows, zoom_factor * grid_rows, gx)
    y_cells = col_start + jnp.arange(cols, dtype=jnp.int32)
    y_tab = table(y_cells, NA // 4, NA, zoom_factor * grid_cols, 1)
    e_new, h_new, *sd = yee(e_field, h_field, material, eps_table, src_pos, src_amp)
    turn_re, turn_im = jnp.cos(1.5 * freqs), jnp.sin(1.5 * freqs)
    half_re, half_im = jnp.cos(0.5 * freqs), jnp.sin(0.5 * freqs)
    mix = jnp.stack(
        [turn_re * half_re, turn_im * half_re, -turn_im * half_im, turn_re * half_im], 1
    )
    group = 4
    inv_norm = 1.0 / math.sqrt(grid_rows * grid_cols)
    fars = []
    for sent in sd:
        got = lax.all_to_all(sent, "gx", split_axis=0, concat_axis=0, tiled=True)
        g = pl.pallas_call(
            rows_kernel,
            grid=(gx // group,),
            out_shape=jax.ShapeDtypeStruct((gx, NF, 2, nu, wide), bf16),
            in_specs=[
                SM,
                pl.BlockSpec((group, 2, nu, grid_rows), lambda i: (i, 0, 0, 0)),
                pl.BlockSpec((gx, rows, 2 * wide), lambda i: (0, 0, 0)),
            ],
            out_specs=pl.BlockSpec((group, NF, 2, nu, wide), lambda i: (i, 0, 0, 0, 0)),
            compiler_params=pltpu.CompilerParams(vmem_limit_bytes=BIG),
            name="rows",
        )(mix, x_tab, got)
        moved = lax.all_to_all(g, "gx", split_axis=0, concat_axis=0, tiled=True)
        share = pl.pallas_call(
            cols_kernel,
            grid=(gy,),
            out_shape=jax.ShapeDtypeStruct((gy, NF * EACH, 2, nu, vb), bf16),
            in_specs=[
                pl.BlockSpec((gx, NF, 2, nu, wide), lambda j: (0, 0, 0, 0, 0)),
                pl.BlockSpec((1, 2, cols, vb), lambda j: (0, 0, 0, j)),
            ],
            out_specs=pl.BlockSpec((1, NF * EACH, 2, nu, vb), lambda j: (j, 0, 0, 0, 0)),
            scratch_shapes=[pltpu.VMEM((2, NF * EACH * nu, cols), bf16)],
            compiler_params=pltpu.CompilerParams(vmem_limit_bytes=BIG),
            cost_estimate=pl.CostEstimate(
                flops=16 * NF * EACH * nu * cols * NA, bytes_accessed=16 * nu * NA, transcendentals=0
            ),
            name="cols",
        )(moved, y_tab)
        summed = lax.psum_scatter(share, "gy", scatter_dimension=0, tiled=True)
        scaled = summed[0].astype(jnp.float32) * inv_norm
        fars.append(jnp.transpose(scaled, (2, 0, 1, 3)).reshape(nu, NF, EACH, 2, vb))
    far = jnp.concatenate(fars, 2).reshape(nu, NF * 4, 2, vb)
    shape = e_field.shape
    return (e_new.reshape(shape), h_new.reshape(shape), far)


def solution(mesh):
    placed = (
        P(None, None, "gx", "gy"),
        P(None, None, "gx", "gy"),
        P(None, "gx", "gy"),
        P(),
        P(),
        P(),
        P(),
    )
    return jax.shard_map(
        on_device,
        mesh=mesh,
        in_specs=placed,
        out_specs=(P(None, None, "gx", "gy"), P(None, None, "gx", "gy"), P("gx", None, None, "gy")),
        check_vma=False,
    )
```
